512 devices in a mesh: pages: 128 (over x, z, core), mp: 4 (over y).
Axes of the slice: x: 4, y: 4, z: 16, core: 2. Of those that a mesh axis runs over, the one named last changes fastest.
Arguments:
- queries: bfloat16 [256, 8192], P('pages', 'mp'), may hold values from -9 to 9
- cached_keys: bfloat16 [2048, 128, 8, 128], P('pages', None, 'mp'), may hold values from -8 to 8
- cached_values: bfloat16 [2048, 128, 8, 128], P('pages', None, 'mp'), may hold values from -4 to 4
- out_weight: bfloat16 [8192, 8192], P('mp', 'pages'), may hold values from -0.0625 to 0.0625
- select: int32 [2, 24], replicated, may hold values from 0 to 2047, as said below
- page_table: int32 [2048], replicated, may hold values from 0 to 2047, as said below
- block_page: int32 [2], replicated, may hold values from 0 to 2047, as said below
Outputs:
- mixed: bfloat16 [256, 8192], P('mp', 'pages')
The draws below stay inside these ranges and needn't reach their ends.
Inputs may be any that keep to these rules, and one draw needn't show every extreme that they name: A permutation: each logical page has its own cache row, held by index page_table[p] // 16 of pages. `select`: each row holds 24 distinct pages: the block's own page block_page[b] and pages lying wholly before the block. They lie on exactly 4 owners, 6 on each. No owner holds selected pages of more than min(2, 4) blocks, and some owner holds that many. `block_page`: Distinct.
All inputs are finite; a program needn't handle non-finite values.
Results may differ from the reference program's by a relative error of at most 0.0063.
Values may be sent and summed in bfloat16 or wider, within the bound.
A program may use at most 64 MiB of HBM per device.

```python
import jax
import jax.numpy as jnp
from jax import lax

D = 8192
QUERY_HEADS = 64
KEY_VALUE_HEADS = 8
HEAD_SIZE = 128
PAGE_TOKENS = 128
PAGES_PER_INDEX = 16
PICKED_PAGES = 6
OWNERS_SEL = 4
QBLOCKS = 2
CACHE_PAGES = 2048
N_PAGES = 128


def page_layout(key):
    owners = N_PAGES
    early = PAGES_PER_INDEX * 7 // 8
    late = PAGES_PER_INDEX - early
    perm_early = jax.random.permutation(jax.random.fold_in(key, 11), owners * early).astype(jnp.int32)
    slot_early = perm_early // early * PAGES_PER_INDEX + perm_early % early
    perm_late = jax.random.permutation(jax.random.fold_in(key, 12), owners * late).astype(jnp.int32)
    slot_late = perm_late // late * PAGES_PER_INDEX + early + perm_late % late
    table = jnp.concatenate([slot_early, slot_late]).astype(jnp.int32)
    inverse = jnp.argsort(table, stable=True).astype(jnp.int32)
    span = min(QBLOCKS + 2, owners)
    half_owners = owners // 2
    base = jax.random.permutation(jax.random.fold_in(key, 13), half_owners)[:span // 2].astype(jnp.int32)
    pool = jnp.stack([base, base + half_owners], axis=1).reshape(-1).astype(jnp.int32)
    position = (jnp.arange(QBLOCKS, dtype=jnp.int32)[:, None] + jnp.arange(OWNERS_SEL, dtype=jnp.int32)[None, :]) % span
    owner_ids = pool[position]
    own_late = jax.random.randint(jax.random.fold_in(key, 14), (QBLOCKS,), 0, late, dtype=jnp.int32)
    block_page = inverse[owner_ids[:, 0] * PAGES_PER_INDEX + early + own_late]
    scores = jax.random.randint(jax.random.fold_in(key, 15), (QBLOCKS, OWNERS_SEL, early), 0, 1 << 20, dtype=jnp.int32) * early + jnp.arange(early, dtype=jnp.int32)
    picks = jnp.argsort(scores, axis=-1, stable=True)[..., :PICKED_PAGES].astype(jnp.int32)
    early_pages = inverse[owner_ids[..., None] * PAGES_PER_INDEX + picks]
    chosen = jnp.concatenate([block_page[:, None], early_pages[:, 0, 1:], early_pages[:, 1:].reshape(QBLOCKS, -1)], axis=1)
    width = OWNERS_SEL * PICKED_PAGES
    mixing = jax.random.randint(jax.random.fold_in(key, 16), (QBLOCKS, width), 0, 1 << 20, dtype=jnp.int32) * width + jnp.arange(width, dtype=jnp.int32)
    shuffle = jnp.argsort(mixing, axis=-1, stable=True)
    chosen = jnp.take_along_axis(chosen, shuffle, axis=1)
    return (table, chosen.astype(jnp.int32), block_page.astype(jnp.int32))


def draw_page_table(key, part):
    return page_layout(key)[0]


def draw_select(key, part):
    return page_layout(key)[1]


def draw_block_page(key, part):
    return page_layout(key)[2]


def draw_queries(key, part):
    count = QBLOCKS * PAGE_TOKENS
    base = jnp.clip(jax.random.normal(jax.random.fold_in(key, 1), (count, QUERY_HEADS, HEAD_SIZE), jnp.float32), -4.0, 4.0)
    return base.reshape(count, QUERY_HEADS * HEAD_SIZE).astype(jnp.bfloat16)


def draw_cached_keys(key, part):
    array_shape = (PAGES_PER_INDEX * N_PAGES, PAGE_TOKENS, KEY_VALUE_HEADS, HEAD_SIZE)
    base = jnp.clip(jax.random.normal(jax.random.fold_in(key, 5), array_shape, jnp.float32), -4.0, 4.0)
    return base.astype(jnp.bfloat16)


def shard_levels(rng, extent, cuts, smallest, largest):
    def one(dim, shards_of):
        heights = jax.random.uniform(jax.random.fold_in(jax.random.fold_in(rng, 6), dim), (shards_of,), jnp.float32, smallest / len(cuts), largest / len(cuts))
        return jnp.repeat(jnp.exp(heights), extent[dim] // shards_of).reshape((-1,) + (1,) * (len(extent) - dim - 1))

    factor_of = one(*cuts[0])
    for cut in cuts[1:]:
        factor_of = factor_of * one(*cut)
    return factor_of


def noise(rng, dims, deviation, bound, shards=(), kind=jnp.bfloat16):
    entries = deviation * jax.random.normal(rng, dims, jnp.float32)
    if shards:
        entries = entries * shard_levels(rng, dims, shards, -0.22, 0.18)
    return jnp.clip(entries, -bound, bound).astype(kind)


def setup_inputs(seed: int = 0) -> dict:
    key_of = jax.random.split(jax.random.key(seed), 8)
    queries = draw_queries(jax.random.fold_in(key_of[7], 71), 0)
    cached_keys = draw_cached_keys(jax.random.fold_in(key_of[7], 71), 0)
    cached_values = noise(key_of[2], (CACHE_PAGES, PAGE_TOKENS, KEY_VALUE_HEADS, HEAD_SIZE), 1.0, 4.0, ((0, 128), (2, 4)))
    out_weight = noise(key_of[3], (QUERY_HEADS * HEAD_SIZE, D), (QUERY_HEADS * HEAD_SIZE) ** -0.5, 0.0625, ((0, 4), (1, 128)))
    select = draw_select(jax.random.fold_in(key_of[7], 71), 0)
    page_table = draw_page_table(jax.random.fold_in(key_of[7], 71), 0)
    block_page = draw_block_page(jax.random.fold_in(key_of[7], 71), 0)
    return dict(queries=queries, cached_keys=cached_keys, cached_values=cached_values, out_weight=out_weight, select=select, page_table=page_table, block_page=block_page)


FLOOR = -1.0e30


def group_attend(row_list, key_rows, value_rows, key_pos, query_pos):
    repeat_heads = QUERY_HEADS // KEY_VALUE_HEADS
    query_block = row_list.astype(jnp.float32).reshape(PAGE_TOKENS, KEY_VALUE_HEADS, repeat_heads, HEAD_SIZE)
    scores = jnp.einsum("rgeh,kgh->rgek", query_block, key_rows.astype(jnp.float32), precision=lax.Precision.HIGHEST) * (HEAD_SIZE ** -0.5)
    allowed = key_pos[None, :] <= query_pos[:, None]
    scores = jnp.where(allowed[:, None, None, :], scores, FLOOR)
    peak = jnp.max(scores, axis=-1)
    weights = jnp.exp(scores - peak[..., None])
    total = jnp.sum(weights, axis=-1)
    rounded = lax.optimization_barrier(weights.astype(jnp.bfloat16)).astype(jnp.float32)
    output = jnp.einsum("rgek,kgh->rgeh", rounded, value_rows.astype(jnp.float32), precision=lax.Precision.HIGHEST)
    return output.reshape(PAGE_TOKENS, QUERY_HEADS, HEAD_SIZE), peak.reshape(PAGE_TOKENS, QUERY_HEADS), total.reshape(PAGE_TOKENS, QUERY_HEADS)


def reference(queries, cached_keys, cached_values, out_weight, select, page_table, block_page):
    offsets = jnp.arange(PAGE_TOKENS, dtype=jnp.int32)
    blocks = []
    for block in range(QBLOCKS):
        row_list = queries[block * PAGE_TOKENS:(block + 1) * PAGE_TOKENS]
        chosen = select[block]
        owners = page_table[chosen] // PAGES_PER_INDEX
        grouped = chosen[jnp.argsort(owners, stable=True)].reshape(OWNERS_SEL, PICKED_PAGES)
        query_pos = block_page[block] * PAGE_TOKENS + offsets
        results = []
        for group in range(OWNERS_SEL):
            pages = grouped[group]
            slot_list = page_table[pages]
            key_rows = cached_keys[slot_list].reshape(PICKED_PAGES * PAGE_TOKENS, KEY_VALUE_HEADS, HEAD_SIZE)
            value_rows = cached_values[slot_list].reshape(PICKED_PAGES * PAGE_TOKENS, KEY_VALUE_HEADS, HEAD_SIZE)
            key_pos = (pages[:, None] * PAGE_TOKENS + offsets[None, :]).reshape(-1).astype(jnp.int32)
            results.append(group_attend(row_list, key_rows, value_rows, key_pos, query_pos))
        row_max = results[0][1]
        for result in results[1:]:
            row_max = jnp.maximum(row_max, result[1])
        row_total = jnp.zeros((PAGE_TOKENS, QUERY_HEADS), jnp.float32)
        for result in results:
            row_total = row_total + result[2] * jnp.exp(result[1] - row_max)
        merged = jnp.zeros((PAGE_TOKENS, QUERY_HEADS, HEAD_SIZE), jnp.float32)
        for output, peak, total in results:
            share = output * (jnp.exp(peak - row_max) / row_total)[..., None]
            merged = merged + lax.optimization_barrier(share.astype(jnp.bfloat16)).astype(jnp.float32)
        blocks.append(merged.astype(jnp.bfloat16).reshape(PAGE_TOKENS, QUERY_HEADS * HEAD_SIZE))
    attention = jnp.concatenate(blocks, axis=0)
    return jnp.dot(attention, out_weight, preferred_element_type=jnp.float32).astype(jnp.bfloat16)
```

```python
import functools

import jax
import jax.numpy as jnp
from jax import lax
from jax.experimental import pallas as pl
from jax.experimental.pallas import tpu as pltpu
from jax.sharding import Mesh
from jax.sharding import PartitionSpec as P

PAGES = ("x", "z", "c")
MESH = pl.DeviceIdType.MESH
NX, NZ, NY = 4, 16, 4
PAGE = 128
PAGES_DEV = 16
PICKED = 6
BLOCKS = 2
HEADS = 8
HEAD = 128
SCALE = HEAD ** -0.5
FLOOR = -1e30
RIGHT = NZ // 2
LEFT = NZ // 2 - 1
VMEM = pltpu.MemorySpace.VMEM
DMA = pltpu.SemaphoreType.DMA


def around(value, size):
    return lax.rem(value + size, size)


def place():
    return tuple(lax.axis_index(axis) for axis in ("x", "z", "c", "y"))


def greet(peers):
    barrier = pltpu.get_barrier_semaphore()
    for peer in peers:
        pl.semaphore_signal(barrier, inc=1, device_id=peer, device_id_type=MESH)
    pl.semaphore_wait(barrier, len(peers))


def sent(source, target, send_sem, recv_sem, peer):
    copy = pltpu.make_async_remote_copy(
        src_ref=source,
        dst_ref=target,
        send_sem=send_sem,
        recv_sem=recv_sem,
        device_id=peer,
        device_id_type=MESH,
    )
    return copy


def spread(buffer, own, x, z, zs_r, zr_r, zs_l, zr_l, xs, xr):
    zr, zl = {"z": around(z + 1, NZ)}, {"z": around(z - 1, NZ)}
    started = []

    def along(slot, step, send, recv, peer):
        copy = sent(buffer.at[x, slot], buffer.at[x, slot], send.at[step], recv.at[step], peer)
        copy.start()
        started.append(copy)

    def across(slot, number):
        for j in range(1, NX):
            copy = sent(
                buffer.at[x, slot],
                buffer.at[x, slot],
                xs.at[j - 1, number],
                xr.at[j - 1, number],
                {"x": around(x + j, NX)},
            )
            copy.start()
            started.append(copy)

    def arrived(slot, sem):
        pltpu.make_async_copy(buffer.at[x, slot], buffer.at[x, slot], sem).wait()

    along(z, 0, zs_r, zr_r, zr)
    along(z, 0, zs_l, zr_l, zl)
    across(z, 0)
    for step in range(RIGHT):
        slot = around(z - 1 - step, NZ)
        arrived(slot, zr_r.at[step])
        if step + 1 < RIGHT:
            along(slot, step + 1, zs_r, zr_r, zr)
        across(slot, 1 + step)
        if step < LEFT:
            slot = around(z + 1 + step, NZ)
            arrived(slot, zr_l.at[step])
            if step + 1 < LEFT:
                along(slot, step + 1, zs_l, zr_l, zl)
            across(slot, 1 + RIGHT + step)
    for j in range(1, NX):
        far = around(x - j, NX)
        for number in range(NZ):
            if number == 0:
                slot = z
            elif number <= RIGHT:
                slot = around(z - number, NZ)
            else:
                slot = around(z + number - RIGHT, NZ)
            sem = xr.at[j - 1, number]
            pltpu.make_async_copy(buffer.at[far, slot], buffer.at[far, slot], sem).wait()
    return started


def collect_kernel(q, k, v, w, qall, kp, vp, wcat, ps, pr, ls, zs_r, zr_r, zs_l, zr_l, xs, xr):
    x, z, c, y = place()
    other = {"c": 1 - c}
    greet([other, {"z": around(z + 1, NZ)}, {"z": around(z - 1, NZ)}] + [{"x": around(x + j, NX)} for j in range(1, NX)])
    pair = [
        sent(q.at[1 - c], qall.at[x, z, c], ps.at[0], pr.at[0], other),
        sent(k, kp, ps.at[1], pr.at[1], other),
        sent(v, vp, ps.at[2], pr.at[2], other),
        sent(w.at[:, pl.ds((1 - c) * 1024, 1024)], wcat.at[c], ps.at[3], pr.at[3], other),
    ]
    mine = pltpu.make_async_copy(q.at[c], qall.at[x, z, c], ls.at[0])
    mine_w = pltpu.make_async_copy(w.at[:, pl.ds(c * 1024, 1024)], wcat.at[c], ls.at[1])
    pair[0].start()
    mine.start()
    for copy in pair[1:]:
        copy.start()
    mine_w.start()
    mine.wait()
    pltpu.make_async_copy(q.at[c], qall.at[x, z, 1 - c], pr.at[0]).wait()
    started = spread(qall, None, x, z, zs_r, zr_r, zs_l, zr_l, xs, xr)
    pltpu.make_async_copy(k, kp, pr.at[1]).wait()
    pltpu.make_async_copy(v, vp, pr.at[2]).wait()
    pltpu.make_async_copy(w.at[:, pl.ds(0, 1024)], wcat.at[1 - c], pr.at[3]).wait()
    mine_w.wait()
    for copy in pair + started:
        copy.wait_send()


SPREAD_SEMS = [DMA((RIGHT,)), DMA((RIGHT,)), DMA((LEFT,)), DMA((LEFT,)), DMA((NX - 1, NZ)), DMA((NX - 1, NZ))]


def collect(q, k, v, w):
    anywhere = pl.BlockSpec(memory_space=pl.ANY)
    inside = pl.BlockSpec(memory_space=VMEM)
    return pl.pallas_call(
        collect_kernel,
        out_shape=(
            jax.ShapeDtypeStruct((NX, NZ, 2, 16, HEAD), jnp.bfloat16),
            jax.ShapeDtypeStruct(k.shape, k.dtype),
            jax.ShapeDtypeStruct(v.shape, v.dtype),
            jax.ShapeDtypeStruct((2, 64, 1024), jnp.bfloat16),
        ),
        in_specs=[inside, anywhere, anywhere, anywhere],
        out_specs=(inside, anywhere, anywhere, anywhere),
        scratch_shapes=[DMA((4,)), DMA((4,)), DMA((2,))] + SPREAD_SEMS,
        compiler_params=pltpu.CompilerParams(collective_id=0, has_side_effects=True),
        name="collect",
    )(q, k, v, w)


def attend_kernel(
    select, table, block_page, q, ko, vo, kp, vp, out, stat,
    listed, counts, kraw, vraw, flat, keys, values, acc, tops, totals, ks, vs,
):
    x, z, c, y = place()
    chip = (x * NZ + z) * 2
    for block in range(BLOCKS):
        own_page = block_page[block]
        own_owner = lax.shift_right_logical(table[own_page], 4)
        for side in range(2):
            owner = chip + jnp.where(side == 0, c, 1 - c)
            first = jnp.where(own_owner == owner, 1, 0)

            def scan(i, n, block=block, side=side, owner=owner, own_page=own_page):
                page = select[block, i]
                row = table[page]
                hit = lax.shift_right_logical(row, 4) == owner
                at = jnp.where(page == own_page, 0, jnp.minimum(n, PICKED - 1))

                @pl.when(hit)
                def _():
                    listed[(block * 2 + side) * PICKED + at] = row & (PAGES_DEV - 1)

                return n + jnp.where(jnp.logical_and(hit, page != own_page), 1, 0)

            filled = lax.fori_loop(0, 4 * PICKED, scan, first)
            counts[block * 2 + side] = filled

            @pl.when(filled == PICKED)
            def _(block=block, side=side):
                combo = block * 2 + side
                for i in range(PICKED):
                    row = listed[combo * PICKED + i]
                    pltpu.make_async_copy((ko, kp)[side].at[row], kraw.at[combo, i], ks.at[combo, i]).start()
                    pltpu.make_async_copy((vo, vp)[side].at[row], vraw.at[combo, i], vs.at[combo, i]).start()

    spot = lax.broadcasted_iota(jnp.int32, (8, HEAD), 1)
    for block in range(BLOCKS):
        any_here = jnp.logical_or(counts[block * 2] == PICKED, counts[block * 2 + 1] == PICKED)
        lines = slice(block * 8, block * 8 + 8)

        @pl.when(jnp.logical_not(any_here))
        def _(lines=lines):
            out[:, lines] = jnp.zeros((NX, 8, 16, 256), jnp.bfloat16)
            stat[:, lines] = jnp.full((NX, 8, 8, HEAD), FLOOR, jnp.float32)

        @pl.when(any_here)
        def _(block=block, lines=lines):
            acc[...] = jnp.zeros(acc.shape, jnp.float32)
            tops[...] = jnp.full(tops.shape, FLOOR, jnp.float32)
            totals[...] = jnp.zeros(totals.shape, jnp.float32)
            for side in range(2):
                combo = block * 2 + side

                @pl.when(counts[combo] == PICKED)
                def _(side=side, combo=combo):
                    for i in range(PICKED):
                        pltpu.make_async_copy(ko.at[0], kraw.at[combo, i], ks.at[combo, i]).wait()
                        flat[...] = kraw[combo, i].astype(jnp.float32)
                        keys[pl.ds(i * PAGE, PAGE), :] = flat[pl.ds(c, PAGE, stride=2), :].astype(jnp.bfloat16)
                    for i in range(PICKED):
                        pltpu.make_async_copy(vo.at[0], vraw.at[combo, i], vs.at[combo, i]).wait()
                        flat[...] = vraw[combo, i].astype(jnp.float32)
                        values[pl.ds(i * PAGE, PAGE), :] = flat[pl.ds(c, PAGE, stride=2), :].astype(jnp.bfloat16)
                    own_owner = lax.shift_right_logical(table[block_page[block]], 4)
                    masked = own_owner == chip + jnp.where(side == 0, c, 1 - c)
                    slack = jnp.where(masked, 0, PAGE)

                    for part in range(4):
                        size = 256
                        rows = pl.ds(part * size, size)
                        qx = 2 * block + part // 2
                        queries = q[qx, (part % 2) * 8:(part % 2) * 8 + 8].reshape(size, HEAD)
                        scores = lax.dot_general(
                            queries, keys[...], (((1,), (1,)), ((), ())), preferred_element_type=jnp.float32
                        ) * SCALE
                        row = lax.broadcasted_iota(jnp.int32, (size, PAGE), 0) // HEADS + part * (size // HEADS)
                        key = lax.broadcasted_iota(jnp.int32, (size, PAGE), 1)
                        head = jnp.where(key <= row + slack, scores[:, :PAGE], FLOOR)
                        scores = jnp.concatenate([head, scores[:, PAGE:]], axis=1)
                        peak = jnp.max(scores, axis=1, keepdims=True)
                        weights = jnp.exp(scores - peak)
                        total = jnp.sum(weights, axis=1, keepdims=True)
                        got = jnp.dot(weights.astype(jnp.bfloat16), values[...], preferred_element_type=jnp.float32)
                        old = tops[rows, :]
                        new = jnp.maximum(old, peak)
                        keep = jnp.exp(old - new)
                        fresh = jnp.exp(peak - new)
                        tops[rows, :] = new
                        totals[rows, :] = totals[rows, :] * keep + total * fresh
                        acc[rows, :] = acc[rows, :] * keep + got * fresh

            acc[...] = acc[...] / totals[...]
            tops[...] = tops[...] + jnp.log(totals[...])
            for xd in range(NX):
                pieces = []
                for half in range(2):
                    head = 2 * xd + half
                    got = acc[pl.ds(head, PAGE, stride=HEADS), :].astype(jnp.bfloat16)
                    out[xd, lines, :, half * HEAD:(half + 1) * HEAD] = got.reshape(8, 16, HEAD)
                    top = tops[pl.ds(head, PAGE, stride=HEADS), :].reshape(8, 16, HEAD)
                    pieces.append(top)
                lane = spot[None]
                low = jnp.where(lane < 32, pieces[0][:, :8], pieces[1][:, :8])
                high = jnp.where(lane < 96, pieces[0][:, 8:], pieces[1][:, 8:])
                stat[xd, lines] = jnp.where(lane < 64, low, high)


def attend(select, table, block_page, q, ko, vo, kp, vp):
    anywhere = pl.BlockSpec(memory_space=pl.ANY)
    inside = pl.BlockSpec(memory_space=VMEM)
    scalars = pl.BlockSpec(memory_space=pltpu.MemorySpace.SMEM)
    combos = BLOCKS * 2
    return pl.pallas_call(
        attend_kernel,
        out_shape=(
            jax.ShapeDtypeStruct((NX, NZ, 16, 256), jnp.bfloat16),
            jax.ShapeDtypeStruct((NX, NZ, 8, HEAD), jnp.float32),
        ),
        in_specs=[scalars] * 3 + [inside] + [anywhere] * 4,
        out_specs=(inside, inside),
        scratch_shapes=[
            pltpu.SMEM((combos * PICKED,), jnp.int32),
            pltpu.SMEM((combos,), jnp.int32),
            pltpu.VMEM((combos, PICKED, 2 * PAGE, HEAD), jnp.bfloat16),
            pltpu.VMEM((combos, PICKED, 2 * PAGE, HEAD), jnp.bfloat16),
            pltpu.VMEM((2 * PAGE, HEAD), jnp.float32),
            pltpu.VMEM((PICKED * PAGE, HEAD), jnp.bfloat16),
            pltpu.VMEM((PICKED * PAGE, HEAD), jnp.bfloat16),
            pltpu.VMEM((PAGE * HEADS, HEAD), jnp.float32),
            pltpu.VMEM((PAGE * HEADS, HEAD), jnp.float32),
            pltpu.VMEM((PAGE * HEADS, HEAD), jnp.float32),
            DMA((combos, PICKED)),
            DMA((combos, PICKED)),
        ],
        name="attend",
    )(select, table, block_page, q, ko, vo, kp, vp)


def blended(items):
    top = items[0][1]
    for _, level in items[1:]:
        top = jnp.maximum(top, level)
    shares = [jnp.exp(level - top) for _, level in items]
    total = shares[0]
    for share in shares[1:]:
        total = total + share
    scale = 1.0 / total
    lines = [[None, None], [None, None]]
    for (value, _), share in zip(items, shares):
        share = share * scale
        for band in range(2):
            for half in range(2):
                lane = band * 64 + half * 32
                term = value[band * 8:(band + 1) * 8, half * HEAD:(half + 1) * HEAD] * share[:, lane:lane + 1]
                before = lines[band][half]
                lines[band][half] = term if before is None else before + term
    value = jnp.concatenate([jnp.concatenate(line, axis=1) for line in lines], axis=0)
    return value, top + jnp.log(total)


def merge_kernel(
    part, stat, w, result, got, got_stat, send_r, send_l, stat_r, stat_l, land_r, land_l, lstat_r, lstat_l,
    chunk, merged, terms, terms_in, sums, sums_in,
    gs, gr, hs, hr, rs, rr, rts, rtr, ls, lr, lts, ltr, cs, ys, yr, ps, pr,
    zs_r, zr_r, zs_l, zr_l, xs, xr,
):
    x, z, c, y = place()
    right, left = {"z": around(z + 1, NZ)}, {"z": around(z - 1, NZ)}
    other = {"c": 1 - c}
    xpeers = [{"x": around(x + j, NX)} for j in range(1, NX)]
    ypeers = [{"y": around(y + j, NY)} for j in range(1, NY)]
    greet([right, left, other] + xpeers + ypeers)
    started = []

    def go(copy):
        copy.start()
        started.append(copy)

    for j in range(1, NX):
        xd = around(x + j, NX)
        go(sent(stat.at[xd], got_stat.at[j - 1], hs.at[j - 1], hr.at[j - 1], xpeers[j - 1]))
    order = []
    for step in range(RIGHT):
        order.append(around(z + RIGHT - step, NZ))
        if step < LEFT:
            order.append(around(z - LEFT + step, NZ))
    order.append(z)
    for number, slot in enumerate(order):
        for j in range(1, NX):
            xd = around(x + j, NX)
            go(sent(part.at[xd, slot], got.at[j - 1, slot], gs.at[j - 1, number], gr.at[j - 1, number], xpeers[j - 1]))
    for j in range(NX - 1):
        pltpu.make_async_copy(got_stat.at[j], got_stat.at[j], hr.at[j]).wait()

    def crossed(number):
        slot = order[number]
        items = [(part[x, slot].astype(jnp.float32), stat[x, slot])]
        for j in range(NX - 1):
            pltpu.make_async_copy(got.at[j, slot], got.at[j, slot], gr.at[j, number]).wait()
            items.append((got[j, slot].astype(jnp.float32), got_stat[j, slot]))
        return blended(items)

    def hop(step, value, send, send_stat, land, land_stat, sems, peer):
        if step > 0:
            pltpu.make_async_copy(land.at[step - 1], land.at[step - 1], sems[1].at[step - 1]).wait()
            pltpu.make_async_copy(land_stat.at[step - 1], land_stat.at[step - 1], sems[3].at[step - 1]).wait()
            value = blended([value, (land[step - 1].astype(jnp.float32), land_stat[step - 1])])
        send[step] = value[0].astype(jnp.bfloat16)
        send_stat[step] = value[1]
        go(sent(send.at[step], land.at[step], sems[0].at[step], sems[1].at[step], peer))
        go(sent(send_stat.at[step], land_stat.at[step], sems[2].at[step], sems[3].at[step], peer))

    number = 0
    for step in range(RIGHT):
        value = crossed(number)
        number += 1
        if step < LEFT:
            second = crossed(number)
            number += 1
        hop(step, value, send_r, stat_r, land_r, lstat_r, (rs, rr, rts, rtr), right)
        if step < LEFT:
            hop(step, second, send_l, stat_l, land_l, lstat_l, (ls, lr, lts, ltr), left)
    items = [crossed(number)]
    for land, land_stat, sem, sem_stat, last in (
        (land_r, lstat_r, rr, rtr, RIGHT - 1),
        (land_l, lstat_l, lr, ltr, LEFT - 1),
    ):
        pltpu.make_async_copy(land.at[last], land.at[last], sem.at[last]).wait()
        pltpu.make_async_copy(land_stat.at[last], land_stat.at[last], sem_stat.at[last]).wait()
        items.append((land[last].astype(jnp.float32), land_stat[last]))
    chunk[...] = blended(items)[0].astype(jnp.bfloat16)
    mine = pltpu.make_async_copy(chunk, merged.at[x, z], cs)
    mine.start()
    mine.wait()
    started.extend(spread(merged, None, x, z, zs_r, zr_r, zs_l, zr_l, xs, xr))
    weight = w[...].reshape(128, 1024)
    total = None
    for xd in range(NX):
        term = lax.dot_general(
            merged[xd].reshape(256, 256),
            weight[:, xd * 256:(xd + 1) * 256],
            (((1,), (1,)), ((), ())),
            preferred_element_type=jnp.float32,
        )
        total = term if total is None else total + term
    terms[...] = total.reshape(NY, 64, 128)
    for j in range(1, NY):
        go(sent(terms.at[around(y + j, NY)], terms_in.at[j - 1], ys.at[j - 1], yr.at[j - 1], ypeers[j - 1]))
    total = terms[y]
    for j in range(NY - 1):
        pltpu.make_async_copy(terms_in.at[j], terms_in.at[j], yr.at[j]).wait()
        total = total + terms_in[j]
    sums[...] = total
    go(sent(sums, sums_in, ps, pr, other))
    pltpu.make_async_copy(sums_in, sums_in, pr).wait()
    total = sums[...] + sums_in[...]
    result[...] = jnp.where(c == 0, total[:, :64], total[:, 64:]).astype(jnp.bfloat16)
    for copy in started:
        copy.wait_send()


def merge(part, stat, w):
    inside = pl.BlockSpec(memory_space=VMEM)
    small = lambda n: pltpu.VMEM((n, 16, 256), jnp.bfloat16)
    level = lambda n: pltpu.VMEM((n, 8, HEAD), jnp.float32)
    return pl.pallas_call(
        merge_kernel,
        out_shape=jax.ShapeDtypeStruct((64, 64), jnp.bfloat16),
        in_specs=[inside] * 3,
        out_specs=inside,
        scratch_shapes=[
            pltpu.VMEM((NX - 1, NZ, 16, 256), jnp.bfloat16),
            pltpu.VMEM((NX - 1, NZ, 8, HEAD), jnp.float32),
            small(RIGHT), small(LEFT), level(RIGHT), level(LEFT),
            small(RIGHT), small(LEFT), level(RIGHT), level(LEFT),
            pltpu.VMEM((16, 256), jnp.bfloat16),
            pltpu.VMEM((NX, NZ, 16, 256), jnp.bfloat16),
            pltpu.VMEM((NY, 64, 128), jnp.float32),
            pltpu.VMEM((NY - 1, 64, 128), jnp.float32),
            pltpu.VMEM((64, 128), jnp.float32),
            pltpu.VMEM((64, 128), jnp.float32),
            DMA((NX - 1, NZ)), DMA((NX - 1, NZ)), DMA((NX - 1,)), DMA((NX - 1,)),
            DMA((RIGHT,)), DMA((RIGHT,)), DMA((RIGHT,)), DMA((RIGHT,)),
            DMA((LEFT,)), DMA((LEFT,)), DMA((LEFT,)), DMA((LEFT,)),
            DMA, DMA((NY - 1,)), DMA((NY - 1,)), DMA, DMA,
        ] + SPREAD_SEMS,
        compiler_params=pltpu.CompilerParams(collective_id=1, has_side_effects=True),
        name="merge",
    )(part, stat, w)


def per_device(queries, cached_keys, cached_values, out_weight, select, page_table, block_page):
    q = queries.reshape(2, 2, HEADS, HEAD).transpose(1, 0, 2, 3).reshape(2, 16, HEAD)
    k = cached_keys.reshape(PAGES_DEV, 2 * PAGE, HEAD)
    v = cached_values.reshape(PAGES_DEV, 2 * PAGE, HEAD)
    qall, kp, vp, wcat = collect(q, k, v, out_weight.T)
    part, stat = attend(select, page_table, block_page, qall, k, v, kp, vp)
    return merge(part, stat, wcat)


def solution(mesh):
    torus = Mesh(mesh.devices.reshape(NX, NZ, 2, NY), ("x", "z", "c", "y"))
    return jax.shard_map(
        per_device,
        mesh=torus,
        in_specs=(
            P(PAGES, "y"),
            P(PAGES, None, "y", None),
            P(PAGES, None, "y", None),
            P("y", PAGES),
            P(),
            P(),
            P(),
        ),
        out_specs=P("y", PAGES),
        check_vma=False,
    )
```

```python
import functools

import jax
import jax.numpy as jnp
from jax import lax
from jax.experimental import pallas as pl
from jax.experimental.pallas import tpu as pltpu
from jax.sharding import Mesh
from jax.sharding import PartitionSpec as P

PAGES = ("x", "z", "c")
MESH = pl.DeviceIdType.MESH
NX, NZ, NY = 4, 16, 4
PAGE = 128
PAGES_DEV = 16
PICKED = 6
BLOCKS = 2
HEADS = 8
HEAD = 128
SCALE = HEAD ** -0.5
FLOOR = -1e30
VMEM = pltpu.MemorySpace.VMEM
DMA = pltpu.SemaphoreType.DMA


def around(value, size):
    return lax.rem(value + size, size)


def place():
    return tuple(lax.axis_index(axis) for axis in ("x", "z", "c", "y"))


def greet(peers):
    barrier = pltpu.get_barrier_semaphore()
    for peer in peers:
        pl.semaphore_signal(barrier, inc=1, device_id=peer, device_id_type=MESH)
    pl.semaphore_wait(barrier, len(peers))


def sent(source, target, send_sem, recv_sem, peer):
    copy = pltpu.make_async_remote_copy(
        src_ref=source,
        dst_ref=target,
        send_sem=send_sem,
        recv_sem=recv_sem,
        device_id=peer,
        device_id_type=MESH,
    )
    return copy


def nearest(reverse=False):
    found = [hop for step in range(1, NZ // 2) for hop in (step, NZ - step)] + [NZ // 2]
    return found[::-1] if reverse else found


def arrived(target, sem):
    pltpu.make_async_copy(target, target, sem).wait()


def across(buffer, slot, number, xs, xr, x, started):
    for j in range(1, NX):
        copy = sent(
            buffer.at[x, slot], buffer.at[x, slot], xs.at[j - 1, number], xr.at[j - 1, number], {"x": around(x + j, NX)}
        )
        copy.start()
        started.append(copy)


def crossed(buffer, slot, number, xr, x):
    for j in range(1, NX):
        arrived(buffer.at[around(x - j, NX), slot], xr.at[j - 1, number])


def collect_kernel(
    select, table, block_page, q, k, v, w, lists, qall, kp, vp, wp, ps, pr, ls, zs, zr, xs, xr
):
    x, z, c, y = place()
    other = {"c": 1 - c}
    peers = [other] + [{"x": around(x + j, NX)} for j in range(1, NX)]
    for hop in nearest(True):
        for core in range(2):
            peers.append({"z": around(z + hop, NZ), "c": core})
    greet(peers)
    started = []

    def go(copy):
        copy.start()
        started.append(copy)

    for hop in nearest(True):
        for core in range(2):
            peer = {"z": around(z + hop, NZ), "c": core}
            go(sent(q.at[core], qall.at[x, z, c], zs.at[hop, core], zr.at[hop, c], peer))
    go(sent(q.at[1 - c], qall.at[x, z, c], zs.at[0, 0], zr.at[0, c], other))
    mine = pltpu.make_async_copy(q.at[c], qall.at[x, z, c], ls)
    mine.start()
    go(sent(k, kp, ps.at[0], pr.at[0], other))
    go(sent(v, vp, ps.at[1], pr.at[1], other))
    go(sent(w.at[:, pl.ds((1 - c) * 1024, 1024)], wp, ps.at[2], pr.at[2], other))
    mine.wait()
    arrived(qall.at[x, z, 1 - c], zr.at[0, 1 - c])
    across(qall, z, 0, xs, xr, x, started)
    chip = x * NZ + z
    for block in range(BLOCKS):
        own_page = block_page[block]
        own_row = table[own_page]
        own_chip = lax.shift_right_logical(own_row, 5)
        for side in range(2):
            core = c if side == 0 else 1 - c
            owner = chip * 2 + core
            has_own = (lax.shift_right_logical(own_row, 4) == owner).astype(jnp.int32)
            count = has_own
            spots = [jnp.where(has_own == 1, own_row & (PAGES_DEV - 1), 0)] + [0] * (PICKED - 1)

            def scan(i, carry, block=block, owner=owner, own_page=own_page):
                count, *spots = carry
                page = select[block, i]
                row = table[page]
                hit = jnp.logical_and(lax.shift_right_logical(row, 4) == owner, page != own_page)
                spots = [
                    jnp.where(jnp.logical_and(hit, count == n), row & (PAGES_DEV - 1), spot)
                    for n, spot in enumerate(spots)
                ]
                return (count + hit.astype(jnp.int32), *spots)

            spots = [jnp.int32(0) + spot for spot in spots]
            count, *spots = lax.fori_loop(0, 4 * PICKED, scan, (count, *spots))
            base = (block * 2 + side) * 8
            for n, spot in enumerate(spots):
                lists[base + n] = spot
            lists[base + PICKED] = count
            lists[base + PICKED + 1] = has_own
    for number, hop in enumerate(nearest()):
        slot = around(z - hop, NZ)
        arrived(qall.at[x, slot, 0], zr.at[hop, 0])
        arrived(qall.at[x, slot, 1], zr.at[hop, 1])
        across(qall, slot, 1 + number, xs, xr, x, started)
    for number, hop in enumerate([0] + nearest()):
        crossed(qall, around(z - hop, NZ), number, xr, x)
    arrived(kp, pr.at[0])
    arrived(vp, pr.at[1])
    arrived(wp, pr.at[2])
    for copy in started:
        copy.wait_send()


X_SEMS = [DMA((NX - 1, NZ)), DMA((NX - 1, NZ))]


def collect(select, table, block_page, q, k, v, w):
    anywhere = pl.BlockSpec(memory_space=pl.ANY)
    inside = pl.BlockSpec(memory_space=VMEM)
    scalars = pl.BlockSpec(memory_space=pltpu.MemorySpace.SMEM)
    return pl.pallas_call(
        collect_kernel,
        out_shape=(
            jax.ShapeDtypeStruct((BLOCKS * 2 * 8,), jnp.int32),
            jax.ShapeDtypeStruct((NX, NZ, 2, 16, HEAD), jnp.bfloat16),
            jax.ShapeDtypeStruct(k.shape, k.dtype),
            jax.ShapeDtypeStruct(v.shape, v.dtype),
            jax.ShapeDtypeStruct((64, 1024), jnp.bfloat16),
        ),
        in_specs=[scalars] * 3 + [inside, anywhere, anywhere, anywhere],
        out_specs=(scalars, inside, anywhere, anywhere, anywhere),
        scratch_shapes=[DMA((3,)), DMA((3,)), DMA, DMA((NZ, 2)), DMA((NZ, 2))] + X_SEMS,
        compiler_params=pltpu.CompilerParams(collective_id=0, has_side_effects=True),
        name="collect",
    )(select, table, block_page, q, k, v, w)


def attend_kernel(lists, q, ko, vo, kp, vp, out, stat, kraw, vraw, flat, keys, values, acc, tops, ks, vs):
    x, z, c, y = place()
    for combo in range(BLOCKS * 2):

        @pl.when(lists[combo * 8 + PICKED] == PICKED)
        def _(combo=combo):
            for i in range(PICKED):
                row = lists[combo * 8 + i]
                pltpu.make_async_copy((ko, kp)[combo % 2].at[row], kraw.at[combo, i], ks.at[combo, i]).start()
            for i in range(PICKED):
                row = lists[combo * 8 + i]
                pltpu.make_async_copy((vo, vp)[combo % 2].at[row], vraw.at[combo, i], vs.at[combo, i]).start()

    def unit(block, side, join):
        combo = block * 2 + side
        for i in range(PICKED):
            pltpu.make_async_copy(ko.at[0], kraw.at[combo, i], ks.at[combo, i]).wait()
            flat[i] = kraw[combo, i].astype(jnp.float32)
            keys[pl.ds(i * PAGE, PAGE), :] = flat[i, pl.ds(c, PAGE, stride=2), :].astype(jnp.bfloat16)
        for i in range(PICKED):
            pltpu.make_async_copy(vo.at[0], vraw.at[combo, i], vs.at[combo, i]).wait()
            flat[i] = vraw[combo, i].astype(jnp.float32)
            values[pl.ds(i * PAGE, PAGE), :] = flat[i, pl.ds(c, PAGE, stride=2), :].astype(jnp.bfloat16)
        slack = jnp.where(lists[combo * 8 + PICKED + 1] == 1, 0, PAGE)
        size = 256
        for part in range(PAGE * HEADS // size):
            rows = pl.ds(part * size, size)
            qx, qz = 2 * block + part // 2, part % 2 * 8
            queries = q[qx, qz:qz + 8].reshape(size, HEAD)
            scores = lax.dot_general(
                queries, keys[...], (((1,), (1,)), ((), ())), preferred_element_type=jnp.float32
            )
            line = lax.broadcasted_iota(jnp.int32, (size, PAGE), 0) + part * size
            row = lax.shift_left(lax.shift_right_logical(line, 4), 1) + (line & 1)
            key = lax.broadcasted_iota(jnp.int32, (size, PAGE), 1)
            head = jnp.where(key <= row + slack, scores[:, :PAGE], FLOOR)
            scores = jnp.concatenate([head, scores[:, PAGE:]], axis=1)
            peak = jnp.max(scores, axis=1, keepdims=True)
            weights = jnp.exp((scores - peak) * SCALE)
            total = jnp.sum(weights, axis=1, keepdims=True)
            got = jnp.dot(weights.astype(jnp.bfloat16), values[...], preferred_element_type=jnp.float32)
            got = got / total
            top = jnp.broadcast_to(peak * SCALE + jnp.log(total), (size, HEAD))
            if join:
                old = tops[rows, :]
                new = jnp.maximum(old, top)
                keep = jnp.exp(old - new)
                fresh = jnp.exp(top - new)
                total = keep + fresh
                got = (acc[rows, :] * keep + got * fresh) / total
                top = new + jnp.log(total)
            tops[rows, :] = top
            acc[rows, :] = got

    lane = lax.broadcasted_iota(jnp.int32, (4, 8, HEAD), 2)
    for block in range(BLOCKS):
        near = lists[block * 16 + PICKED] == PICKED
        far = lists[block * 16 + 8 + PICKED] == PICKED
        lines = slice(block * 8, block * 8 + 8)

        @pl.when(jnp.logical_not(jnp.logical_or(near, far)))
        def _(lines=lines):
            out[:, lines] = jnp.zeros((NX, 8, 16, 256), jnp.bfloat16)
            stat[:, lines] = jnp.full((NX, 8, 8, HEAD), FLOOR, jnp.float32)

        @pl.when(near)
        def _(block=block):
            unit(block, 0, False)

        @pl.when(jnp.logical_and(far, jnp.logical_not(near)))
        def _(block=block):
            unit(block, 1, False)

        @pl.when(jnp.logical_and(far, near))
        def _(block=block):
            unit(block, 1, True)

        @pl.when(jnp.logical_or(near, far))
        def _(block=block):
            for xd in range(NX):
                for r in range(2):
                    here = slice(block * 8 + r * 4, block * 8 + r * 4 + 4)
                    pieces = []
                    for half in range(2):
                        start = (2 * xd + half) * 2 + r
                        got = acc[pl.ds(start, 64, stride=16), :].astype(jnp.bfloat16)
                        out[xd, here, :, half * HEAD:(half + 1) * HEAD] = got.reshape(4, 16, HEAD)
                        pieces.append(tops[pl.ds(start, 64, stride=16), :].reshape(4, 16, HEAD))
                    low = jnp.where(lane < 32, pieces[0][:, :8], pieces[1][:, :8])
                    high = jnp.where(lane < 96, pieces[0][:, 8:], pieces[1][:, 8:])
                    stat[xd, here] = jnp.where(lane < 64, low, high)


def attend(lists, q, ko, vo, kp, vp):
    anywhere = pl.BlockSpec(memory_space=pl.ANY)
    inside = pl.BlockSpec(memory_space=VMEM)
    scalars = pl.BlockSpec(memory_space=pltpu.MemorySpace.SMEM)
    combos = BLOCKS * 2
    return pl.pallas_call(
        attend_kernel,
        out_shape=(
            jax.ShapeDtypeStruct((NX, NZ, 16, 256), jnp.bfloat16),
            jax.ShapeDtypeStruct((NX, NZ, 8, HEAD), jnp.float32),
        ),
        in_specs=[scalars, inside] + [anywhere] * 4,
        out_specs=(inside, inside),
        scratch_shapes=[
            pltpu.VMEM((combos, PICKED, 2 * PAGE, HEAD), jnp.bfloat16),
            pltpu.VMEM((combos, PICKED, 2 * PAGE, HEAD), jnp.bfloat16),
            pltpu.VMEM((PICKED, 2 * PAGE, HEAD), jnp.float32),
            pltpu.VMEM((PICKED * PAGE, HEAD), jnp.bfloat16),
            pltpu.VMEM((PICKED * PAGE, HEAD), jnp.bfloat16),
            pltpu.VMEM((PAGE * HEADS, HEAD), jnp.float32),
            pltpu.VMEM((PAGE * HEADS, HEAD), jnp.float32),
            DMA((combos, PICKED)),
            DMA((combos, PICKED)),
        ],
        name="attend",
    )(lists, q, ko, vo, kp, vp)


def blended(items):
    top = items[0][1]
    for _, level in items[1:]:
        top = jnp.maximum(top, level)
    shares = [jnp.exp(level - top) for _, level in items]
    total = shares[0]
    for share in shares[1:]:
        total = total + share
    scale = 1.0 / total
    lines = [[None, None], [None, None]]
    for (value, _), share in zip(items, shares):
        share = share * scale
        for band in range(2):
            for half in range(2):
                lane = band * 64 + half * 32
                term = value[band * 8:(band + 1) * 8, half * HEAD:(half + 1) * HEAD] * share[:, lane:lane + 1]
                before = lines[band][half]
                lines[band][half] = term if before is None else before + term
    value = jnp.concatenate([jnp.concatenate(line, axis=1) for line in lines], axis=0)
    return value, top + jnp.log(total)


def merge_kernel(
    part, stat, w, wp, result, got, got_stat, send, send_stat, land, land_stat, wcat,
    chunk, merged, terms, terms_in, sums, sums_in, lines,
    gs, gr, hs, hr, rs, rr, ts, tr, cs, ys, yr, ps, pr, zs, zr, xs, xr,
):
    x, z, c, y = place()
    other = {"c": 1 - c}
    xpeers = [{"x": around(x + j, NX)} for j in range(1, NX)]
    ypeers = [{"y": around(y + j, NY)} for j in range(1, NY)]
    zpeers = {hop: {"z": around(z + hop, NZ)} for hop in range(1, NZ)}
    greet([other] + xpeers + ypeers + [zpeers[hop] for hop in nearest(True)])
    started = []

    def go(copy):
        copy.start()
        started.append(copy)

    for j in range(1, NX):
        xd = around(x + j, NX)
        go(sent(stat.at[xd], got_stat.at[j - 1], hs.at[j - 1], hr.at[j - 1], xpeers[j - 1]))
    order = nearest(True) + [0]
    for number, hop in enumerate(order):
        slot = around(z + hop, NZ)
        for j in range(1, NX):
            xd = around(x + j, NX)
            go(sent(part.at[xd, slot], got.at[j - 1, slot], gs.at[j - 1, number], gr.at[j - 1, number], xpeers[j - 1]))
    wcat[c] = w[:, pl.ds(pl.multiple_of(c * 1024, 1024), 1024)]
    wcat[1 - c] = wp[...]
    for j in range(NX - 1):
        arrived(got_stat.at[j], hr.at[j])
    own = None
    for number, hop in enumerate(order):
        slot = around(z + hop, NZ)
        items = [(part[x, slot].astype(jnp.float32), stat[x, slot])]
        for j in range(NX - 1):
            arrived(got.at[j, slot], gr.at[j, number])
            items.append((got[j, slot].astype(jnp.float32), got_stat[j, slot]))
        value, level = blended(items)
        if hop == 0:
            own = value, level
        else:
            send[hop - 1] = value.astype(jnp.bfloat16)
            send_stat[hop - 1] = level
            go(sent(send_stat.at[hop - 1], land_stat.at[hop - 1], ts.at[hop - 1], tr.at[hop - 1], zpeers[hop]))
            go(sent(send.at[hop - 1], land.at[hop - 1], rs.at[hop - 1], rr.at[hop - 1], zpeers[hop]))
    items = [own]
    for hop in nearest():
        arrived(land_stat.at[hop - 1], tr.at[hop - 1])
        arrived(land.at[hop - 1], rr.at[hop - 1])
        items.append((land[hop - 1].astype(jnp.float32), land_stat[hop - 1]))
    chunk[...] = blended(items)[0].astype(jnp.bfloat16)
    for hop in nearest(True):
        go(sent(chunk, merged.at[x, z], zs.at[hop], zr.at[hop], zpeers[hop]))
    mine = pltpu.make_async_copy(chunk, merged.at[x, z], cs)
    mine.start()
    mine.wait()
    across(merged, z, 0, xs, xr, x, started)
    for number, hop in enumerate(nearest()):
        slot = around(z - hop, NZ)
        arrived(merged.at[x, slot], zr.at[hop])
        across(merged, slot, 1 + number, xs, xr, x, started)
    for number, hop in enumerate([0] + nearest()):
        crossed(merged, around(z - hop, NZ), number, xr, x)
    weight = wcat[...].reshape(128, 1024)
    total = None
    for xd in range(NX):
        term = lax.dot_general(
            merged[xd].reshape(256, 256),
            weight[:, xd * 256:(xd + 1) * 256],
            (((1,), (1,)), ((), ())),
            preferred_element_type=jnp.float32,
        )
        total = term if total is None else total + term
    total = total.reshape(2, 2, 2, 32, 128)
    for block in range(2):
        for near in range(2):
            terms[block * 2 + near] = total[block, :, near]
    for j in range(1, NY):
        go(sent(terms.at[around(y + j, NY)], terms_in.at[j - 1], ys.at[j - 1], yr.at[j - 1], ypeers[j - 1]))
    total = terms[y]
    for j in range(NY - 1):
        arrived(terms_in.at[j], yr.at[j])
        total = total + terms_in[j]
    sums[...] = total
    go(sent(sums, sums_in, ps, pr, other))
    arrived(sums_in, pr)
    total = sums[...] + sums_in[...]
    for r in range(2):
        lines[pl.ds(r, 32, stride=2), :] = total[r]
    total = lines[...]
    result[...] = jnp.where(c == 0, total[:, :64], total[:, 64:]).astype(jnp.bfloat16)
    for copy in started:
        copy.wait_send()


def merge(part, stat, w, wp):
    inside = pl.BlockSpec(memory_space=VMEM)
    piece = pltpu.VMEM((NZ - 1, 16, 256), jnp.bfloat16)
    level = pltpu.VMEM((NZ - 1, 8, HEAD), jnp.float32)
    return pl.pallas_call(
        merge_kernel,
        out_shape=jax.ShapeDtypeStruct((64, 64), jnp.bfloat16),
        in_specs=[inside] * 4,
        out_specs=inside,
        scratch_shapes=[
            pltpu.VMEM((NX - 1, NZ, 16, 256), jnp.bfloat16),
            pltpu.VMEM((NX - 1, NZ, 8, HEAD), jnp.float32),
            piece, level, piece, level,
            pltpu.VMEM((2, 64, 1024), jnp.bfloat16),
            pltpu.VMEM((16, 256), jnp.bfloat16),
            pltpu.VMEM((NX, NZ, 16, 256), jnp.bfloat16),
            pltpu.VMEM((NY, 2, 32, 128), jnp.float32),
            pltpu.VMEM((NY - 1, 2, 32, 128), jnp.float32),
            pltpu.VMEM((2, 32, 128), jnp.float32),
            pltpu.VMEM((2, 32, 128), jnp.float32),
            pltpu.VMEM((64, 128), jnp.float32),
            DMA((NX - 1, NZ)), DMA((NX - 1, NZ)), DMA((NX - 1,)), DMA((NX - 1,)),
            DMA((NZ - 1,)), DMA((NZ - 1,)), DMA((NZ - 1,)), DMA((NZ - 1,)),
            DMA, DMA((NY - 1,)), DMA((NY - 1,)), DMA, DMA, DMA((NZ,)), DMA((NZ,)),
        ] + X_SEMS,
        compiler_params=pltpu.CompilerParams(collective_id=1, has_side_effects=True),
        name="merge",
    )(part, stat, w, wp)


def per_device(queries, cached_keys, cached_values, out_weight, select, page_table, block_page):
    q = queries.reshape(2, 2 * HEADS, HEAD).transpose(1, 0, 2).reshape(2, 16, HEAD)
    k = cached_keys.reshape(PAGES_DEV, 2 * PAGE, HEAD)
    v = cached_values.reshape(PAGES_DEV, 2 * PAGE, HEAD)
    w = out_weight.T
    lists, qall, kp, vp, wp = collect(select, page_table, block_page, q, k, v, w)
    part, stat = attend(lists, qall, k, v, kp, vp)
    return merge(part, stat, w, wp)


def solution(mesh):
    torus = Mesh(mesh.devices.reshape(NX, NZ, 2, NY), ("x", "z", "c", "y"))
    return jax.shard_map(
        per_device,
        mesh=torus,
        in_specs=(
            P(PAGES, "y"),
            P(PAGES, None, "y", None),
            P(PAGES, None, "y", None),
            P("y", PAGES),
            P(),
            P(),
            P(),
        ),
        out_specs=P("y", PAGES),
        check_vma=False,
    )
```

```python
import jax
import jax.numpy as jnp
from jax import lax
from jax.experimental import pallas as pl
from jax.experimental.pallas import tpu as pltpu
from jax.sharding import Mesh
from jax.sharding import PartitionSpec as P

PAGES = ("x", "z", "c")
MESH = pl.DeviceIdType.MESH
NX, NZ, NY = 4, 16, 4
PAGE = 128
PAGES_DEV = 16
PICKED = 6
BLOCKS = 2
HEADS = 8
HEAD = 128
KEYS = PICKED * PAGE
SCALE = HEAD ** -0.5
FLOOR = -1e30
VMEM = pltpu.MemorySpace.VMEM
DMA = pltpu.SemaphoreType.DMA
TERM = jnp.bfloat16


def around(value, size):
    return lax.rem(value + size, size)


def place():
    return tuple(lax.axis_index(axis) for axis in ("x", "z", "c", "y"))


def greet(peers):
    barrier = pltpu.get_barrier_semaphore()
    for peer in peers:
        pl.semaphore_signal(barrier, inc=1, device_id=peer, device_id_type=MESH)
    pl.semaphore_wait(barrier, len(peers))


def sent(source, target, send_sem, recv_sem, peer):
    return pltpu.make_async_remote_copy(
        src_ref=source,
        dst_ref=target,
        send_sem=send_sem,
        recv_sem=recv_sem,
        device_id=peer,
        device_id_type=MESH,
    )


def arrived(target, sem):
    pltpu.make_async_copy(target, target, sem).wait()


def nearest(reverse=False):
    found = [hop for step in range(1, NZ // 2) for hop in (step, NZ - step)] + [NZ // 2]
    return found[::-1] if reverse else found


def blended(items):
    top = items[0][1]
    for _, level in items[1:]:
        top = jnp.maximum(top, level)
    shares = [jnp.exp(level - top) for _, level in items]
    total = shares[0]
    for share in shares[1:]:
        total = total + share
    scale = 1.0 / total
    lines = [[None, None], [None, None]]
    for (value, _), share in zip(items, shares):
        share = share * scale
        for band in range(2):
            for half in range(2):
                lane = band * 64 + half * 32
                term = value[band * 8:(band + 1) * 8, half * HEAD:(half + 1) * HEAD] * share[:, lane:lane + 1]
                before = lines[band][half]
                lines[band][half] = term if before is None else before + term
    value = jnp.concatenate([jnp.concatenate(line, axis=1) for line in lines], axis=0)
    return value, top + jnp.log(total)


def listed(select, table, block_page, lists, chip, c):
    for block in range(BLOCKS):
        own_page = block_page[block]
        own_row = table[own_page]
        for side in range(2):
            owner = chip * 2 + (c if side == 0 else 1 - c)
            has_own = (lax.shift_right_logical(own_row, 4) == owner).astype(jnp.int32)
            spots = [jnp.where(has_own == 1, own_row & (PAGES_DEV - 1), 0)] + [jnp.int32(0)] * (PICKED - 1)

            def scan(i, carry, block=block, owner=owner, own_page=own_page):
                count, *spots = carry
                page = select[block, i]
                row = table[page]
                hit = jnp.logical_and(lax.shift_right_logical(row, 4) == owner, page != own_page)
                spots = [
                    jnp.where(jnp.logical_and(hit, count == n), row & (PAGES_DEV - 1), spot)
                    for n, spot in enumerate(spots)
                ]
                return (count + hit.astype(jnp.int32), *spots)

            count, *spots = lax.fori_loop(0, 4 * PICKED, scan, (has_own, *spots))
            base = (block * 2 + side) * 8
            for n, spot in enumerate(spots):
                lists[base + n] = spot
            lists[base + PICKED] = count
            lists[base + PICKED + 1] = has_own


def step_kernel(
    select, table, block_page, q, k, v, w, result,
    lists, qall, knear, vnear, kfar, vfar, flat, keys, values, acc, tops, part, stat, got, got_stat,
    send, send_stat, land, land_stat, merged, wz, terms, terms_in, lines,
    ls, ps, pr, zs, zr, xs, xr, ws, wr, gs, gr, hs, hr, rs, rr, ts, tr, ms, mr, fs, fr,
):
    x, z, c, y = place()
    here = x * 2 + c
    other = {"c": 1 - c}
    xpeers = [{"x": around(x + j, NX)} for j in range(1, NX)]
    near = [{"x": around(x + j, NX), "c": lax.rem(c + d, 2)} for j in range(NX) for d in range(2)][1:]
    zero = jnp.zeros((2 * NX, 64, 256), jnp.bfloat16)
    wz[:, :64, 256:] = zero
    wz[:, 64:, :256] = zero
    peers = [{"z": around(z + hop, NZ), "c": core} for hop in nearest(True) for core in range(2)] + near
    for j in range(1, NY):
        for peer in [{"x": x, "c": c}] + near:
            peers.append({"y": around(y + j, NY), **peer})
    own = [
        pltpu.make_async_copy(k, knear, ls.at[0]),
        pltpu.make_async_copy(v, vnear, ls.at[1]),
        pltpu.make_async_copy(q.at[c], qall.at[x, z, c], ls.at[2]),
    ]
    mine = pl.multiple_of((c * NX + x) * 256, 256)
    for n in range(2):
        own.append(pltpu.make_async_copy(
            w.at[:, pl.ds(mine, 256)], wz.at[here, pl.ds(64 * n, 64), pl.ds(256 * n, 256)], ls.at[3 + n]
        ))
    for copy in own:
        copy.start()
    greet(peers)
    started = []

    def go(copy):
        copy.start()
        started.append(copy)

    for hop in nearest(True):
        for core in range(2):
            peer = {"z": around(z + hop, NZ), "c": core}
            go(sent(q.at[core], qall.at[x, z, c], zs.at[hop, core], zr.at[hop, c], peer))
    go(sent(q.at[1 - c], qall.at[x, z, c], zs.at[0, 0], zr.at[0, c], other))
    go(sent(k, kfar, ps.at[0], pr.at[0], other))
    go(sent(v, vfar, ps.at[1], pr.at[1], other))

    def across(slot, number):
        for j in range(1, NX):
            go(sent(qall.at[x, slot], qall.at[x, slot], xs.at[j - 1, number], xr.at[j - 1, slot], xpeers[j - 1]))

    listed(select, table, block_page, lists, x * NZ + z, c)
    for copy in own:
        copy.wait()
    arrived(qall.at[x, z, 1 - c], zr.at[0, 1 - c])
    across(z, 0)

    def untangle(side, raws):
        def one(i, _, side=side):
            for block in range(BLOCKS):
                row = lists[(block * 2 + side) * 8 + i]
                at = pl.ds(pl.multiple_of(i * PAGE, PAGE), PAGE)
                for n, (raw, kept) in enumerate(zip(raws, (keys, values))):
                    spot = block * 2 + n
                    flat[spot] = raw[row].astype(jnp.float32)
                    kept[block * 2 + side, at, :] = flat[spot, pl.ds(c, PAGE, stride=2), :].astype(jnp.bfloat16)
            return 0

        lax.fori_loop(0, PICKED, one, 0)

    untangle(0, (knear, vnear))
    for number, hop in enumerate(nearest()):
        slot = around(z - hop, NZ)
        arrived(qall.at[x, slot, 0], zr.at[hop, 0])
        arrived(qall.at[x, slot, 1], zr.at[hop, 1])
        across(slot, 1 + number)
    for number, peer in enumerate(near):
        xd, cd = peer["x"], peer["c"]
        theirs = pl.multiple_of((cd * NX + xd) * 256, 256)
        for n in range(2):
            go(sent(
                w.at[:, pl.ds(theirs, 256)],
                wz.at[here, pl.ds(64 * n, 64), pl.ds(256 * n, 256)],
                ws.at[number, n], wr.at[here, n], peer,
            ))
    arrived(kfar, pr.at[0])
    arrived(vfar, pr.at[1])
    untangle(1, (kfar, vfar))
    lane = lax.broadcasted_iota(jnp.int32, (2, 8, HEAD), 2)
    size = 256

    def group(xg):
        block = xg // 2
        away = around(x - xg, NX)

        @pl.when(away != 0)
        def _():
            for slot in range(NZ):
                arrived(qall.at[xg, slot], xr.at[away - 1, slot])

        for tile in range(2):
            rows = pl.ds(tile * size, size)
            queries = qall[xg, tile * 8:tile * 8 + 8].reshape(size, HEAD)
            sides = []
            for side in range(2):
                combo = block * 2 + side
                scores = lax.dot_general(
                    queries, keys[combo], (((1,), (1,)), ((), ())), preferred_element_type=jnp.float32
                )
                slack = jnp.where(lists[combo * 8 + PICKED + 1] == 1, 0, PAGE)
                line = lax.broadcasted_iota(jnp.int32, (size, PAGE), 0) + tile * size
                row = lax.shift_left(lax.shift_right_logical(line, 4), 1) + (line & 1) + xg % 2 * 64
                key = lax.broadcasted_iota(jnp.int32, (size, PAGE), 1)
                first = jnp.where(key <= row + slack, scores[:, :PAGE], FLOOR)
                scores = jnp.concatenate([first, scores[:, PAGE:]], axis=1)
                peak = jnp.max(scores, axis=1, keepdims=True)
                weights = jnp.exp((scores - peak) * SCALE)
                total = jnp.sum(weights, axis=1, keepdims=True)
                out = jnp.dot(weights.astype(jnp.bfloat16), values[combo], preferred_element_type=jnp.float32)
                level = peak * SCALE + jnp.log(total)
                level = jnp.where(lists[combo * 8 + PICKED] == PICKED, level, FLOOR)
                sides.append((out, total, level))
            top = jnp.maximum(sides[0][2], sides[1][2])
            shares = [jnp.exp(level - top) for _, _, level in sides]
            whole = shares[0] + shares[1]
            acc[rows, :] = sum(
                out * (share / (whole * total)) for (out, total, _), share in zip(sides, shares)
            )
            tops[rows, :] = jnp.broadcast_to(top + jnp.log(whole), (size, HEAD))
        for xd in range(NX):
            for r in range(2):
                at = slice(4 * xg + 2 * r, 4 * xg + 2 * r + 2)
                pieces = []
                for half in range(2):
                    start = (2 * xd + half) * 2 + r
                    piece = acc[pl.ds(start, 32, stride=16), :].astype(jnp.bfloat16)
                    part[xd, at, :, half * HEAD:(half + 1) * HEAD] = piece.reshape(2, 16, HEAD)
                    pieces.append(tops[pl.ds(start, 32, stride=16), :].reshape(2, 16, HEAD))
                low = jnp.where(lane < 32, pieces[0][:, :8], pieces[1][:, :8])
                high = jnp.where(lane < 96, pieces[0][:, 8:], pieces[1][:, 8:])
                stat[xd, at] = jnp.where(lane < 64, low, high)
        at = pl.ds(4 * xg, 4)
        for j in range(1, NX):
            xd = around(x + j, NX)
            go(sent(stat.at[xd, at], got_stat.at[j - 1, at], hs.at[j - 1, xg], hr.at[j - 1, xg], xpeers[j - 1]))
            go(sent(part.at[xd, at], got.at[j - 1, at], gs.at[j - 1, xg], gr.at[j - 1, xg], xpeers[j - 1]))

    def along(slot, value, level):
        peer = {"z": jnp.int32(slot)}
        return [
            sent(send_stat.at[slot], land_stat.at[z], ts.at[slot], tr.at[z], peer),
            sent(send.at[slot], land.at[z], rs.at[slot], rr.at[z], peer),
        ]

    def combine(xg):
        at = pl.ds(4 * xg, 4)
        for j in range(NX - 1):
            arrived(got_stat.at[j, at], hr.at[j, xg])
            arrived(got.at[j, at], gr.at[j, xg])
        for slot in range(4 * xg, 4 * xg + 4):
            items = [(part[x, slot].astype(jnp.float32), stat[x, slot])]
            for j in range(NX - 1):
                items.append((got[j, slot].astype(jnp.float32), got_stat[j, slot]))
            value, level = blended(items)

            @pl.when(z == slot)
            def _(value=value, level=level):
                land[z] = value.astype(jnp.bfloat16)
                land_stat[z] = level

            @pl.when(z != slot)
            def _(value=value, level=level, slot=slot):
                send[slot] = value.astype(jnp.bfloat16)
                send_stat[slot] = level
                for copy in along(slot, value, level):
                    copy.start()

    group(0)
    group(1)
    combine(0)
    group(2)
    combine(1)
    group(3)
    combine(2)
    combine(3)
    for hop in nearest():
        slot = around(z - hop, NZ)
        arrived(land_stat.at[slot], tr.at[slot])
        arrived(land.at[slot], rr.at[slot])
    items = [(land[slot].astype(jnp.float32), land_stat[slot]) for slot in range(NZ)]
    merged[z] = blended(items)[0].astype(jnp.bfloat16)
    for hop in nearest(True):
        go(sent(merged.at[z], merged.at[z], ms.at[hop], mr.at[hop], {"z": around(z + hop, NZ)}))
    for number, peer in enumerate(near):
        there = peer["x"] * 2 + peer["c"]
        for n in range(2):
            arrived(wz.at[there, pl.ds(64 * n, 64), pl.ds(256 * n, 256)], wr.at[there, n])
    for hop in nearest():
        arrived(merged.at[around(z - hop, NZ)], mr.at[hop])
    rows = merged[...].reshape(NY, 2, 32, 256)
    rows = jnp.concatenate([rows[:, 0].reshape(128, 256), rows[:, 1].reshape(128, 256)], axis=1)
    for spot in range(2 * NX):
        term = lax.dot_general(rows, wz[spot], (((1,), (1,)), ((), ())), preferred_element_type=jnp.float32)
        terms[spot] = term.reshape(NY, 32, 128).astype(TERM)
    number = 0
    for j in range(NY)[::-1]:
        for peer in ([] if j == 0 else [{"x": x, "c": c}]) + near:
            yd = around(y + j, NY)
            spot = peer["x"] * 2 + peer["c"]
            mark = y * 8 + here
            go(sent(terms.at[spot, yd], terms_in.at[mark], fs.at[number], fr.at[mark], {"y": yd, **peer}))
            number += 1
    total = terms[here, y].astype(jnp.float32)
    for j in range(NY):
        for peer in ([] if j == 0 else [{"x": x, "c": c}]) + near:
            mark = around(y + j, NY) * 8 + peer["x"] * 2 + peer["c"]
            arrived(terms_in.at[mark], fr.at[mark])
            total = total + terms_in[mark].astype(jnp.float32)
    lines[pl.ds(0, 32, stride=2), :] = total
    lines[pl.ds(1, 32, stride=2), :] = jnp.concatenate([total[:, 64:], total[:, :64]], axis=1)
    result[...] = lines[:, :64].astype(jnp.bfloat16)
    for copy in started:
        copy.wait_send()
    for slot in range(NZ):

        @pl.when(z != slot)
        def _(slot=slot):
            for copy in along(slot, None, None):
                copy.wait_send()


def step(select, table, block_page, q, k, v, w):
    anywhere = pl.BlockSpec(memory_space=pl.ANY)
    inside = pl.BlockSpec(memory_space=VMEM)
    scalars = pl.BlockSpec(memory_space=pltpu.MemorySpace.SMEM)
    half = lambda *shape: pltpu.VMEM(shape, jnp.bfloat16)
    full = lambda *shape: pltpu.VMEM(shape, jnp.float32)
    pages = (PAGES_DEV, 2 * PAGE, HEAD)
    return pl.pallas_call(
        step_kernel,
        out_shape=jax.ShapeDtypeStruct((64, 64), jnp.bfloat16),
        in_specs=[scalars] * 3 + [inside] + [anywhere] * 3,
        out_specs=inside,
        scratch_shapes=[
            pltpu.SMEM((BLOCKS * 2 * 8,), jnp.int32),
            half(NX, NZ, 2, 16, HEAD),
            half(*pages), half(*pages), half(*pages), half(*pages),
            full(4, 2 * PAGE, HEAD),
            half(4, KEYS, HEAD), half(4, KEYS, HEAD),
            full(512, HEAD), full(512, HEAD),
            half(NX, NZ, 16, 256), full(NX, NZ, 8, HEAD),
            half(NX - 1, NZ, 16, 256), full(NX - 1, NZ, 8, HEAD),
            half(NZ, 16, 256), full(NZ, 8, HEAD),
            half(NZ, 16, 256), full(NZ, 8, HEAD),
            half(NZ, 16, 256),
            half(2 * NX, 128, 512),
            pltpu.VMEM((2 * NX, NY, 32, 128), TERM),
            pltpu.VMEM((8 * NY, 32, 128), TERM),
            full(64, 128),
            DMA((5,)), DMA((2,)), DMA((2,)),
            DMA((NZ, 2)), DMA((NZ, 2)), DMA((NX - 1, NZ)), DMA((NX - 1, NZ)),
            DMA((7, 2)), DMA((8, 2)),
            DMA((NX - 1, NX)), DMA((NX - 1, NX)), DMA((NX - 1, NX)), DMA((NX - 1, NX)),
            DMA((NZ,)), DMA((NZ,)), DMA((NZ,)), DMA((NZ,)),
            DMA((NZ,)), DMA((NZ,)),
            DMA((31,)), DMA((32,)),
        ],
        compiler_params=pltpu.CompilerParams(collective_id=0, has_side_effects=True),
        name="step",
    )(select, table, block_page, q, k, v, w)


def per_device(queries, cached_keys, cached_values, out_weight, select, page_table, block_page):
    q = queries.reshape(2, 2 * HEADS, HEAD).transpose(1, 0, 2).reshape(2, 16, HEAD)
    k = cached_keys.reshape(PAGES_DEV, 2 * PAGE, HEAD)
    v = cached_values.reshape(PAGES_DEV, 2 * PAGE, HEAD)
    return step(select, page_table, block_page, q, k, v, out_weight.T)


def solution(mesh):
    torus = Mesh(mesh.devices.reshape(NX, NZ, 2, NY), ("x", "z", "c", "y"))
    return jax.shard_map(
        per_device,
        mesh=torus,
        in_specs=(
            P(PAGES, "y"),
            P(PAGES, None, "y", None),
            P(PAGES, None, "y", None),
            P("y", PAGES),
            P(),
            P(),
            P(),
        ),
        out_specs=P("y", PAGES),
        check_vma=False,
    )
```

```python
import jax
import jax.numpy as jnp
from jax import lax
from jax.experimental import pallas as pl
from jax.experimental.pallas import tpu as pltpu
from jax.sharding import Mesh
from jax.sharding import PartitionSpec as P

PAGES = ("x", "z", "c")
MESH = pl.DeviceIdType.MESH
NX, NZ, NY = 4, 16, 4
PAGE = 128
PAGES_DEV = 16
PICKED = 6
BLOCKS = 2
HEADS = 8
HEAD = 128
KEYS = PICKED * PAGE
SCALE = HEAD ** -0.5
FLOOR = -1e30
VMEM = pltpu.MemorySpace.VMEM
DMA = pltpu.SemaphoreType.DMA
TERM = jnp.bfloat16


def around(value, size):
    return lax.rem(value + size, size)


def place():
    return tuple(lax.axis_index(axis) for axis in ("x", "z", "c", "y"))


def greet(peers):
    barrier = pltpu.get_barrier_semaphore()
    for peer in peers:
        pl.semaphore_signal(barrier, inc=1, device_id=peer, device_id_type=MESH)
    return lambda: pl.semaphore_wait(barrier, len(peers))


def sent(source, target, send_sem, recv_sem, peer):
    return pltpu.make_async_remote_copy(
        src_ref=source,
        dst_ref=target,
        send_sem=send_sem,
        recv_sem=recv_sem,
        device_id=peer,
        device_id_type=MESH,
    )


def arrived(target, sem):
    pltpu.make_async_copy(target, target, sem).wait()


def nearest(reverse=False):
    found = [hop for step in range(1, NZ // 2) for hop in (step, NZ - step)] + [NZ // 2]
    return found[::-1] if reverse else found


def weighed(levels):
    top = levels[0]
    for level in levels[1:]:
        top = jnp.maximum(top, level)
    shares = [jnp.exp(level - top) for level in levels]
    total = shares[0]
    for share in shares[1:]:
        total = total + share
    scale = 1.0 / total
    return [share * scale for share in shares], top + jnp.log(total)


def mixed_by(values, shares, base):
    lines = []
    for band in range(2):
        line = []
        for half in range(2):
            lane = base + 8 * (band * 2 + half)
            total = None
            for value, share in zip(values, shares):
                term = value[band * 8:(band + 1) * 8, half * HEAD:(half + 1) * HEAD] * share[:, lane:lane + 1]
                total = term if total is None else total + term
            line.append(total)
        lines.append(jnp.concatenate(line, axis=1))
    return jnp.concatenate(lines, axis=0)


def listed(select, table, block_page, lists, chip, c):
    for block in range(BLOCKS):
        own_page = block_page[block]
        own_row = table[own_page]
        for side in range(2):
            owner = chip * 2 + (c if side == 0 else 1 - c)
            has_own = (lax.shift_right_logical(own_row, 4) == owner).astype(jnp.int32)
            spots = [jnp.where(has_own == 1, own_row & (PAGES_DEV - 1), 0)] + [jnp.int32(0)] * (PICKED - 1)

            def scan(i, carry, block=block, owner=owner, own_page=own_page):
                count, *spots = carry
                page = select[block, i]
                row = table[page]
                hit = jnp.logical_and(lax.shift_right_logical(row, 4) == owner, page != own_page)
                spots = [
                    jnp.where(jnp.logical_and(hit, count == n), row & (PAGES_DEV - 1), spot)
                    for n, spot in enumerate(spots)
                ]
                return (count + hit.astype(jnp.int32), *spots)

            count, *spots = lax.fori_loop(0, 4 * PICKED, scan, (has_own, *spots))
            base = (block * 2 + side) * 8
            for n, spot in enumerate(spots):
                lists[base + n] = spot
            lists[base + PICKED] = count
            lists[base + PICKED + 1] = has_own


def step_kernel(
    select_in, table_in, block_page_in, q_in, k, v, w, result,
    select, table, block_page, lists, q, qall, knear, vnear, kfar, vfar, flat, keys, values, acc, tops,
    part, stat, got, got_stat, send, send_stat, land, land_stat, merged, wz, terms, terms_in, lines,
    ls, ps, pr, zs, zr, xs, xr, ws, wr, gs, gr, hs, hr, rs, rr, ts, tr, ms, mr, fs, fr,
):
    x, z, c, y = place()
    here = x * 2 + c
    other = {"c": 1 - c}
    xpeers = [{"x": around(x + j, NX)} for j in range(1, NX)]
    around_me = [{"x": around(x + j, NX), "c": lax.rem(c + d, 2)} for j in range(NX) for d in range(2)]
    near = around_me[1:]
    peers = [{"z": around(z + hop, NZ), "c": core} for hop in nearest(True) for core in range(2)] + near
    for j in range(1, NY):
        for peer in around_me:
            peers.append({"y": around(y + j, NY), **peer})
    wait_for_all = greet(peers)
    mine = pl.multiple_of((c * NX + x) * 256, 256)
    own = [
        pltpu.make_async_copy(select_in, select, ls.at[0]),
        pltpu.make_async_copy(table_in, table, ls.at[1]),
        pltpu.make_async_copy(block_page_in, block_page, ls.at[2]),
        pltpu.make_async_copy(q_in, q, ls.at[3]),
        pltpu.make_async_copy(k, knear, ls.at[4]),
        pltpu.make_async_copy(v, vnear, ls.at[5]),
        pltpu.make_async_copy(w.at[:, pl.ds(mine, 256)], wz.at[here, pl.ds(0, 64), pl.ds(0, 256)], ls.at[6]),
    ]
    for copy in own:
        copy.start()
    for copy in own[:4]:
        copy.wait()
    copy = pltpu.make_async_copy(q.at[c], qall.at[x, z, c], ls.at[7])
    copy.start()
    zero = jnp.zeros((2 * NX, 64, 256), jnp.bfloat16)
    wz[:, :64, 256:] = zero
    wz[:, 64:, :256] = zero
    listed(select, table, block_page, lists, x * NZ + z, c)
    for copy in own[4:] + [copy]:
        copy.wait()
    started = []

    def go(copy):
        copy.start()
        started.append(copy)

    def across(slot, number):
        for j in range(1, NX):
            go(sent(qall.at[x, slot], qall.at[x, slot], xs.at[j - 1, number], xr.at[j - 1, slot], xpeers[j - 1]))

    def untangle(side, raws):
        def one(i, _, side=side):
            for block in range(BLOCKS):
                row = lists[(block * 2 + side) * 8 + i]
                at = pl.ds(pl.multiple_of(i * PAGE, PAGE), PAGE)
                for n, (raw, kept) in enumerate(zip(raws, (keys, values))):
                    spot = block * 2 + n
                    flat[spot] = raw[row].astype(jnp.float32)
                    kept[block * 2 + side, at, :] = flat[spot, pl.ds(c, PAGE, stride=2), :].astype(jnp.bfloat16)
            return 0

        lax.fori_loop(0, PICKED, one, 0)

    untangle(0, (knear, vnear))
    wait_for_all()
    for hop in nearest(True):
        for core in range(2):
            peer = {"z": around(z + hop, NZ), "c": core}
            go(sent(q.at[core], qall.at[x, z, c], zs.at[hop, core], zr.at[hop, c], peer))
    go(sent(q.at[1 - c], qall.at[x, z, c], zs.at[0, 0], zr.at[0, c], other))
    go(sent(knear, kfar, ps.at[0], pr.at[0], other))
    go(sent(vnear, vfar, ps.at[1], pr.at[1], other))
    for number, peer in enumerate(near):
        theirs = pl.multiple_of((peer["c"] * NX + peer["x"]) * 256, 256)
        target = wz.at[here, pl.ds(0, 64), pl.ds(0, 256)]
        go(sent(w.at[:, pl.ds(theirs, 256)], target, ws.at[number], wr.at[here], peer))
    arrived(qall.at[x, z, 1 - c], zr.at[0, 1 - c])
    across(z, 0)
    for number, hop in enumerate(nearest()):
        slot = around(z - hop, NZ)
        arrived(qall.at[x, slot, 0], zr.at[hop, 0])
        arrived(qall.at[x, slot, 1], zr.at[hop, 1])
        across(slot, 1 + number)
    arrived(kfar, pr.at[0])
    arrived(vfar, pr.at[1])
    untangle(1, (kfar, vfar))
    lane = lax.broadcasted_iota(jnp.int32, (8, HEAD), 1)
    size = 256

    def group(xg):
        block = xg // 2
        away = around(x - xg, NX)

        @pl.when(away != 0)
        def _():
            for slot in range(NZ):
                arrived(qall.at[xg, slot], xr.at[away - 1, slot])

        for tile in range(2):
            rows = pl.ds(tile * size, size)
            queries = qall[xg, tile * 8:tile * 8 + 8].reshape(size, HEAD)
            sides = []
            for side in range(2):
                combo = block * 2 + side
                scores = lax.dot_general(
                    queries, keys[combo], (((1,), (1,)), ((), ())), preferred_element_type=jnp.float32
                )
                slack = jnp.where(lists[combo * 8 + PICKED + 1] == 1, 0, PAGE)
                line = lax.broadcasted_iota(jnp.int32, (size, PAGE), 0) + tile * size
                row = lax.shift_left(lax.shift_right_logical(line, 4), 1) + (line & 1) + xg % 2 * 64
                key = lax.broadcasted_iota(jnp.int32, (size, PAGE), 1)
                first = jnp.where(key <= row + slack, scores[:, :PAGE], FLOOR)
                scores = jnp.concatenate([first, scores[:, PAGE:]], axis=1)
                peak = jnp.max(scores, axis=1, keepdims=True)
                weights = jnp.exp((scores - peak) * SCALE)
                total = jnp.sum(weights, axis=1, keepdims=True)
                out = jnp.dot(weights.astype(jnp.bfloat16), values[combo], preferred_element_type=jnp.float32)
                level = peak * SCALE + jnp.log(total)
                level = jnp.where(lists[combo * 8 + PICKED] == PICKED, level, FLOOR)
                sides.append((out, total, level))
            top = jnp.maximum(sides[0][2], sides[1][2])
            shares = [jnp.exp(level - top) for _, _, level in sides]
            whole = shares[0] + shares[1]
            acc[rows, :] = sum(
                out * (share / (whole * total)) for (out, total, _), share in zip(sides, shares)
            )
            tops[rows, :] = jnp.broadcast_to(top + jnp.log(whole), (size, HEAD))
        for xd in range(NX):
            tile = None
            for r in range(2):
                at = slice(4 * xg + 2 * r, 4 * xg + 2 * r + 2)
                pieces = []
                for half in range(2):
                    start = (2 * xd + half) * 2 + r
                    piece = acc[pl.ds(start, 32, stride=16), :].astype(jnp.bfloat16)
                    part[xd, at, :, half * HEAD:(half + 1) * HEAD] = piece.reshape(2, 16, HEAD)
                    pieces.append(tops[pl.ds(start, 32, stride=16), :])
                for spot in range(8):
                    top = pieces[spot % 2][spot // 2 * 8:spot // 2 * 8 + 8]
                    tile = top if tile is None else jnp.where(lane >= r * 64 + spot * 8, top, tile)
            stat[xd, xg] = tile
        at = pl.ds(4 * xg, 4)
        for j in range(1, NX):
            xd = around(x + j, NX)
            go(sent(stat.at[xd, xg], got_stat.at[j - 1, xg], hs.at[j - 1, xg], hr.at[j - 1, xg], xpeers[j - 1]))
            go(sent(part.at[xd, at], got.at[j - 1, at], gs.at[j - 1, xg], gr.at[j - 1, xg], xpeers[j - 1]))

    def along(slot):
        peer = {"z": jnp.int32(slot)}
        return [
            sent(send_stat.at[slot], land_stat.at[z], ts.at[slot], tr.at[z], peer),
            sent(send.at[slot], land.at[z], rs.at[slot], rr.at[z], peer),
        ]

    def combine(xg):
        for j in range(NX - 1):
            arrived(got_stat.at[j, xg], hr.at[j, xg])
            arrived(got.at[j, pl.ds(4 * xg, 4)], gr.at[j, xg])
        shares, level = weighed([stat[x, xg]] + [got_stat[j, xg] for j in range(NX - 1)])
        for i in range(4):
            slot = 4 * xg + i
            items = [part[x, slot]] + [got[j, slot] for j in range(NX - 1)]
            value = mixed_by([item.astype(jnp.float32) for item in items], shares, 32 * i)
            turned = pltpu.roll(level, 128 - 32 * i, 1) if i else level

            @pl.when(z == slot)
            def _(value=value, turned=turned):
                land[z] = value.astype(jnp.bfloat16)
                land_stat[z] = turned

            @pl.when(z != slot)
            def _(value=value, turned=turned, slot=slot):
                send[slot] = value.astype(jnp.bfloat16)
                send_stat[slot] = turned
                for copy in along(slot):
                    copy.start()

    group(0)
    group(1)
    combine(0)
    group(2)
    combine(1)
    group(3)
    combine(2)
    combine(3)
    for hop in nearest():
        slot = around(z - hop, NZ)
        arrived(land_stat.at[slot], tr.at[slot])
        arrived(land.at[slot], rr.at[slot])
    shares, _ = weighed([land_stat[slot] for slot in range(NZ)])
    merged[z] = mixed_by([land[slot].astype(jnp.float32) for slot in range(NZ)], shares, 0).astype(jnp.bfloat16)
    for hop in nearest(True):
        go(sent(merged.at[z], merged.at[z], ms.at[hop], mr.at[hop], {"z": around(z + hop, NZ)}))
    for peer in near:
        there = peer["x"] * 2 + peer["c"]
        arrived(wz.at[there, pl.ds(0, 64), pl.ds(0, 256)], wr.at[there])
    for spot in range(2 * NX):
        wz[spot, 64:, 256:] = wz[spot, :64, :256]

    def outward(rows_of, number):
        peer = around_me[number]
        spot = peer["x"] * 2 + peer["c"]
        mark = y * 8 + here
        return sent(
            terms.at[spot, rows_of], terms_in.at[mark], fs.at[rows_of, number], fr.at[mark], {"y": rows_of, **peer}
        )

    for turn in (0, 1, 3, 2):
        rows_of = around(lax.div(z, NX) + turn, NY)
        for i in range(4):
            slot = rows_of * 4 + i
            hop = around(z - slot + NZ, NZ)
            if turn == 0:

                @pl.when(hop != 0)
                def _(slot=slot, hop=hop):
                    arrived(merged.at[slot], mr.at[hop])
            else:
                arrived(merged.at[slot], mr.at[hop])
        rows = merged[pl.ds(rows_of * 4, 4)].reshape(2, 32, 256)
        rows = jnp.concatenate([rows[0], rows[1]], axis=1)
        for spot in range(2 * NX):
            term = lax.dot_general(rows, wz[spot], (((1,), (1,)), ((), ())), preferred_element_type=jnp.float32)
            terms[spot, rows_of] = term.astype(TERM)

        @pl.when(rows_of != y)
        def _(rows_of=rows_of):
            outward(rows_of, 0).start()

        for number in range(1, 8):
            outward(rows_of, number).start()
    total = terms[here, y].astype(jnp.float32)
    for j in range(NY):
        for peer in ([] if j == 0 else [{"x": x, "c": c}]) + near:
            mark = around(y + j, NY) * 8 + peer["x"] * 2 + peer["c"]
            arrived(terms_in.at[mark], fr.at[mark])
            total = total + terms_in[mark].astype(jnp.float32)
    lines[pl.ds(0, 32, stride=2), :] = total
    lines[pl.ds(1, 32, stride=2), :] = jnp.concatenate([total[:, 64:], total[:, :64]], axis=1)
    result[...] = lines[:, :64].astype(jnp.bfloat16)
    for copy in started:
        copy.wait_send()
    for rows_of in range(NY):

        @pl.when(rows_of != y)
        def _(rows_of=rows_of):
            outward(rows_of, 0).wait_send()

        for number in range(1, 8):
            outward(rows_of, number).wait_send()
    for slot in range(NZ):

        @pl.when(z != slot)
        def _(slot=slot):
            for copy in along(slot):
                copy.wait_send()


def step(select, table, block_page, q, k, v, w):
    anywhere = pl.BlockSpec(memory_space=pl.ANY)
    inside = pl.BlockSpec(memory_space=VMEM)
    half = lambda *shape: pltpu.VMEM(shape, jnp.bfloat16)
    full = lambda *shape: pltpu.VMEM(shape, jnp.float32)
    pages = (PAGES_DEV, 2 * PAGE, HEAD)
    return pl.pallas_call(
        step_kernel,
        out_shape=jax.ShapeDtypeStruct((64, 64), jnp.bfloat16),
        in_specs=[anywhere] * 7,
        out_specs=inside,
        scratch_shapes=[
            pltpu.SMEM(select.shape, jnp.int32),
            pltpu.SMEM(table.shape, jnp.int32),
            pltpu.SMEM(block_page.shape, jnp.int32),
            pltpu.SMEM((BLOCKS * 2 * 8,), jnp.int32),
            half(2, 16, HEAD),
            half(NX, NZ, 2, 16, HEAD),
            half(*pages), half(*pages), half(*pages), half(*pages),
            full(4, 2 * PAGE, HEAD),
            half(4, KEYS, HEAD), half(4, KEYS, HEAD),
            full(512, HEAD), full(512, HEAD),
            half(NX, NZ, 16, 256), full(NX, NX, 8, HEAD),
            half(NX - 1, NZ, 16, 256), full(NX - 1, NX, 8, HEAD),
            half(NZ, 16, 256), full(NZ, 8, HEAD),
            half(NZ, 16, 256), full(NZ, 8, HEAD),
            half(NZ, 16, 256),
            half(2 * NX, 128, 512),
            pltpu.VMEM((2 * NX, NY, 32, 128), TERM),
            pltpu.VMEM((8 * NY, 32, 128), TERM),
            full(64, 128),
            DMA((8,)), DMA((2,)), DMA((2,)),
            DMA((NZ, 2)), DMA((NZ, 2)), DMA((NX - 1, NZ)), DMA((NX - 1, NZ)),
            DMA((7,)), DMA((8,)),
            DMA((NX - 1, NX)), DMA((NX - 1, NX)), DMA((NX - 1, NX)), DMA((NX - 1, NX)),
            DMA((NZ,)), DMA((NZ,)), DMA((NZ,)), DMA((NZ,)),
            DMA((NZ,)), DMA((NZ,)),
            DMA((NY, 8)), DMA((32,)),
        ],
        compiler_params=pltpu.CompilerParams(collective_id=0, has_side_effects=True),
        name="step",
    )(select, table, block_page, q, k, v, w)


def per_device(queries, cached_keys, cached_values, out_weight, select, page_table, block_page):
    q = queries.reshape(2, 2 * HEADS, HEAD).transpose(1, 0, 2).reshape(2, 16, HEAD)
    k = cached_keys.reshape(PAGES_DEV, 2 * PAGE, HEAD)
    v = cached_values.reshape(PAGES_DEV, 2 * PAGE, HEAD)
    return step(select, page_table, block_page, q, k, v, out_weight.T)


def solution(mesh):
    torus = Mesh(mesh.devices.reshape(NX, NZ, 2, NY), ("x", "z", "c", "y"))
    return jax.shard_map(
        per_device,
        mesh=torus,
        in_specs=(
            P(PAGES, "y"),
            P(PAGES, None, "y", None),
            P(PAGES, None, "y", None),
            P("y", PAGES),
            P(),
            P(),
            P(),
        ),
        out_specs=P("y", PAGES),
        check_vma=False,
    )
```

```python
import jax
import jax.numpy as jnp
from jax import lax
from jax.experimental import pallas as pl
from jax.experimental.pallas import tpu as pltpu
from jax.sharding import Mesh
from jax.sharding import PartitionSpec as P

PAGES = ("x", "z", "c")
MESH = pl.DeviceIdType.MESH
NX, NZ, NY = 4, 16, 4
REACH = NZ // 4
PAGE = 128
PAGES_DEV = 16
PICKED = 6
BLOCKS = 2
HEADS = 8
HEAD = 128
KEYS = PICKED * PAGE
SCALE = HEAD ** -0.5
SCALE2 = SCALE * 1.4426950408889634
FLOOR = -1e30
VMEM = pltpu.MemorySpace.VMEM
DMA = pltpu.SemaphoreType.DMA
TERM = jnp.bfloat16


def around(value, size):
    return lax.rem(value + size, size)


def place():
    return tuple(lax.axis_index(axis) for axis in ("x", "z", "c", "y"))


def greet(peers):
    barrier = pltpu.get_barrier_semaphore()
    for peer in peers:
        pl.semaphore_signal(barrier, inc=1, device_id=peer, device_id_type=MESH)
    return lambda: pl.semaphore_wait(barrier, len(peers))


def sent(source, target, send_sem, recv_sem, peer):
    return pltpu.make_async_remote_copy(
        src_ref=source,
        dst_ref=target,
        send_sem=send_sem,
        recv_sem=recv_sem,
        device_id=peer,
        device_id_type=MESH,
    )


def arrived(target, sem):
    pltpu.make_async_copy(target, target, sem).wait()


def nearest(reverse=False):
    found = [hop for step in range(1, NZ // 2) for hop in (step, NZ - step)] + [NZ // 2]
    return found[::-1] if reverse else found


def weighed(levels):
    top = levels[0]
    for level in levels[1:]:
        top = jnp.maximum(top, level)
    shares = [jnp.exp(level - top) for level in levels]
    total = shares[0]
    for share in shares[1:]:
        total = total + share
    scale = 1.0 / total
    return [share * scale for share in shares], top + jnp.log(total)


def mixed_by(values, shares, base):
    lines = []
    for band in range(2):
        line = []
        for half in range(2):
            lane = base + 8 * (band * 2 + half)
            total = None
            for value, share in zip(values, shares):
                term = value[band * 8:(band + 1) * 8, half * HEAD:(half + 1) * HEAD] * share[:, lane:lane + 1]
                total = term if total is None else total + term
            line.append(total)
        lines.append(jnp.concatenate(line, axis=1))
    return jnp.concatenate(lines, axis=0)


def listed(select, table, block_page, lists, chip, c):
    for block in range(BLOCKS):
        own_page = block_page[block]
        own_row = table[own_page]
        for side in range(2):
            owner = chip * 2 + (c if side == 0 else 1 - c)
            has_own = (lax.shift_right_logical(own_row, 4) == owner).astype(jnp.int32)
            spots = [jnp.where(has_own == 1, own_row & (PAGES_DEV - 1), 0)] + [jnp.int32(0)] * (PICKED - 1)

            def scan(i, carry, block=block, owner=owner, own_page=own_page):
                count, *spots = carry
                page = select[block, i]
                row = table[page]
                hit = jnp.logical_and(lax.shift_right_logical(row, 4) == owner, page != own_page)
                spots = [
                    jnp.where(jnp.logical_and(hit, count == n), row & (PAGES_DEV - 1), spot)
                    for n, spot in enumerate(spots)
                ]
                return (count + hit.astype(jnp.int32), *spots)

            count, *spots = lax.fori_loop(0, 4 * PICKED, scan, (has_own, *spots))
            base = (block * 2 + side) * 8
            for n, spot in enumerate(spots):
                lists[base + n] = spot
            lists[base + PICKED] = count
            lists[base + PICKED + 1] = has_own


def step_kernel(
    select_in, table_in, block_page_in, q_in, k, v, w, result,
    select, table, block_page, lists, q, qall, knear, vnear, kfar, vfar, flat, keys, values, acc, tops,
    part, stat, got, got_stat, send, send_stat, land, land_stat, merged, wz, terms, terms_in, lines,
    ls, ps, pr, zs, zr, xs, xr, ws, wr, gs, gr, hs, hr, rs, rr, ts, tr, ms, mr, fs, fr,
):
    x, z, c, y = place()
    here = x * 2 + c
    other = {"c": 1 - c}
    xpeers = [{"x": around(x + j, NX)} for j in range(1, NX)]
    around_me = [{"x": around(x + j, NX), "c": lax.rem(c + d, 2)} for j in range(NX) for d in range(2)]
    near = around_me[1:]
    close = nearest()[2 * REACH - 1::-1]
    peers = [{"z": around(z + hop, NZ), "c": core} for hop in close for core in range(2)] + near
    for j in range(1, NY):
        for peer in around_me:
            peers.append({"y": around(y + j, NY), **peer})
    wait_for_all = greet(peers)
    mine = pl.multiple_of((c * NX + x) * 256, 256)
    own = [
        pltpu.make_async_copy(select_in, select, ls.at[0]),
        pltpu.make_async_copy(table_in, table, ls.at[1]),
        pltpu.make_async_copy(block_page_in, block_page, ls.at[2]),
        pltpu.make_async_copy(q_in, q, ls.at[3]),
        pltpu.make_async_copy(k, knear, ls.at[4]),
        pltpu.make_async_copy(v, vnear, ls.at[5]),
        pltpu.make_async_copy(w.at[:, pl.ds(mine, 256)], wz.at[here, pl.ds(0, 64), pl.ds(0, 256)], ls.at[6]),
    ]
    for copy in own:
        copy.start()
    own[3].wait()
    copy = pltpu.make_async_copy(q.at[c], qall.at[x, z, c], ls.at[7])
    copy.start()
    own.append(copy)
    started = []

    def go(copy):
        copy.start()
        started.append(copy)

    def across(slot, number):
        for j in range(1, NX):
            go(sent(qall.at[x, slot], qall.at[x, slot], xs.at[j - 1, number], xr.at[j - 1, slot], xpeers[j - 1]))

    def untangle(side, raws):
        def one(i, _, side=side):
            for block in range(BLOCKS):
                row = lists[(block * 2 + side) * 8 + i]
                at = pl.ds(pl.multiple_of(i * PAGE, PAGE), PAGE)
                for n, (raw, kept) in enumerate(zip(raws, (keys, values))):
                    spot = block * 2 + n
                    flat[spot] = raw[row].astype(jnp.float32)
                    kept[block * 2 + side, at, :HEAD] = flat[spot, pl.ds(c, PAGE, stride=2), :].astype(jnp.bfloat16)
            return 0

        lax.fori_loop(0, PICKED, one, 0)

    wait_for_all()
    for hop in close:
        for core in range(2):
            peer = {"z": around(z + hop, NZ), "c": core}
            go(sent(q.at[core], qall.at[x, z, c], zs.at[hop, core], zr.at[hop, c], peer))
    go(sent(q.at[1 - c], qall.at[x, z, c], zs.at[0, 0], zr.at[0, c], other))
    own[4].wait()
    own[5].wait()
    go(sent(knear, kfar, ps.at[0], pr.at[0], other))
    go(sent(vnear, vfar, ps.at[1], pr.at[1], other))
    for number, peer in enumerate(near):
        theirs = pl.multiple_of((peer["c"] * NX + peer["x"]) * 256, 256)
        target = wz.at[here, pl.ds(0, 64), pl.ds(0, 256)]
        go(sent(w.at[:, pl.ds(theirs, 256)], target, ws.at[number], wr.at[here], peer))
    for copy in own[:3] + own[6:]:
        copy.wait()
    def came(hop):
        slot = around(z - hop, NZ)
        for core in range(2):
            arrived(qall.at[x, slot, core], zr.at[hop, core])
        return slot

    for sign in (1, -1):
        slot = came(REACH if sign == 1 else NZ - REACH)
        for leg in range(REACH if sign == 1 else REACH - 1, 0, -1):
            hop = sign * (REACH + leg) % NZ
            go(sent(
                qall.at[x, slot], qall.at[x, slot], zs.at[hop, 0], zr.at[hop, 0], {"z": around(z + sign * leg, NZ)}
            ))
    arrived(qall.at[x, z, 1 - c], zr.at[0, 1 - c])
    across(z, 0)
    for number, hop in enumerate(nearest()[:2 * REACH]):
        if hop in (REACH, NZ - REACH):
            slot = around(z - hop, NZ)
        else:
            slot = came(hop)
        across(slot, 1 + number)
    zero = jnp.zeros((2 * NX, 64, 256), jnp.bfloat16)
    wz[:, :64, 256:] = zero
    wz[:, 64:, :256] = zero
    values[:, :, HEAD:] = jnp.ones((4, KEYS, HEAD), jnp.bfloat16)
    listed(select, table, block_page, lists, x * NZ + z, c)
    untangle(0, (knear, vnear))
    for number, hop in enumerate(nearest()[2 * REACH:]):
        slot = around(z - hop, NZ)
        arrived(qall.at[x, slot], zr.at[hop, 0])
        across(slot, 1 + 2 * REACH + number)
    arrived(kfar, pr.at[0])
    arrived(vfar, pr.at[1])
    untangle(1, (kfar, vfar))
    lane = lax.broadcasted_iota(jnp.int32, (8, HEAD), 1)
    size = 256

    def group(xg):
        block = xg // 2
        away = around(x - xg, NX)

        @pl.when(away != 0)
        def _():
            for slot in range(NZ):
                arrived(qall.at[xg, slot], xr.at[away - 1, slot])

        for tile in range(2):
            rows = pl.ds(tile * size, size)
            queries = qall[xg, tile * 8:tile * 8 + 8].reshape(size, HEAD)
            sides = []
            for side in range(2):
                combo = block * 2 + side
                scores = lax.dot_general(
                    queries, keys[combo], (((1,), (1,)), ((), ())), preferred_element_type=jnp.float32
                )
                slack = jnp.where(lists[combo * 8 + PICKED + 1] == 1, 0, PAGE)
                line = lax.broadcasted_iota(jnp.int32, (size, PAGE), 0) + tile * size
                row = lax.shift_left(lax.shift_right_logical(line, 4), 1) + (line & 1) + xg % 2 * 64
                key = lax.broadcasted_iota(jnp.int32, (size, PAGE), 1)
                first = jnp.where(key <= row + slack, scores[:, :PAGE], FLOOR)
                scores = jnp.concatenate([first, scores[:, PAGE:]], axis=1)
                peak = jnp.max(scores, axis=1, keepdims=True)
                weights = jnp.exp2((scores - peak) * SCALE2)
                both = jnp.dot(weights.astype(jnp.bfloat16), values[combo], preferred_element_type=jnp.float32)
                out, total = both[:, :HEAD], both[:, HEAD:HEAD + 1]
                level = peak * SCALE + jnp.log(total)
                level = jnp.where(lists[combo * 8 + PICKED] == PICKED, level, FLOOR)
                sides.append((out, total, level))
            top = jnp.maximum(sides[0][2], sides[1][2])
            shares = [jnp.exp(level - top) for _, _, level in sides]
            whole = shares[0] + shares[1]
            acc[rows, :] = sum(
                out * (share / (whole * total)) for (out, total, _), share in zip(sides, shares)
            )
            tops[rows, :] = jnp.broadcast_to(top + jnp.log(whole), (size, HEAD))
        for xd in range(NX):
            tile = None
            for r in range(2):
                at = slice(4 * xg + 2 * r, 4 * xg + 2 * r + 2)
                pieces = []
                for half in range(2):
                    start = (2 * xd + half) * 2 + r
                    piece = acc[pl.ds(start, 32, stride=16), :].astype(jnp.bfloat16)
                    part[xd, at, :, half * HEAD:(half + 1) * HEAD] = piece.reshape(2, 16, HEAD)
                    pieces.append(tops[pl.ds(start, 32, stride=16), :])
                for spot in range(8):
                    top = pieces[spot % 2][spot // 2 * 8:spot // 2 * 8 + 8]
                    tile = top if tile is None else jnp.where(lane >= r * 64 + spot * 8, top, tile)
            stat[xd, xg] = tile
        at = pl.ds(4 * xg, 4)
        for j in range(1, NX):
            xd = around(x + j, NX)
            go(sent(stat.at[xd, xg], got_stat.at[j - 1, xg], hs.at[j - 1, xg], hr.at[j - 1, xg], xpeers[j - 1]))
            go(sent(part.at[xd, at], got.at[j - 1, at], gs.at[j - 1, xg], gr.at[j - 1, xg], xpeers[j - 1]))

    def along(slot):
        peer = {"z": jnp.int32(slot)}
        return [
            sent(send_stat.at[slot], land_stat.at[z], ts.at[slot], tr.at[z], peer),
            sent(send.at[slot], land.at[z], rs.at[slot], rr.at[z], peer),
        ]

    def combine(xg):
        for j in range(NX - 1):
            arrived(got_stat.at[j, xg], hr.at[j, xg])
            arrived(got.at[j, pl.ds(4 * xg, 4)], gr.at[j, xg])
        shares, level = weighed([stat[x, xg]] + [got_stat[j, xg] for j in range(NX - 1)])
        for i in range(4):
            slot = 4 * xg + i
            items = [part[x, slot]] + [got[j, slot] for j in range(NX - 1)]
            value = mixed_by([item.astype(jnp.float32) for item in items], shares, 32 * i)
            turned = pltpu.roll(level, 128 - 32 * i, 1) if i else level

            @pl.when(z == slot)
            def _(value=value, turned=turned):
                land[z] = value.astype(jnp.bfloat16)
                land_stat[z] = turned

            @pl.when(z != slot)
            def _(value=value, turned=turned, slot=slot):
                send[slot] = value.astype(jnp.bfloat16)
                send_stat[slot] = turned
                for copy in along(slot):
                    copy.start()

    group(0)
    group(1)
    combine(0)
    group(2)
    combine(1)
    group(3)
    combine(2)
    combine(3)
    for hop in nearest():
        slot = around(z - hop, NZ)
        arrived(land_stat.at[slot], tr.at[slot])
        arrived(land.at[slot], rr.at[slot])
    shares, _ = weighed([land_stat[slot] for slot in range(NZ)])
    merged[z] = mixed_by([land[slot].astype(jnp.float32) for slot in range(NZ)], shares, 0).astype(jnp.bfloat16)
    for hop in nearest(True):
        go(sent(merged.at[z], merged.at[z], ms.at[hop], mr.at[hop], {"z": around(z + hop, NZ)}))
    for peer in near:
        there = peer["x"] * 2 + peer["c"]
        arrived(wz.at[there, pl.ds(0, 64), pl.ds(0, 256)], wr.at[there])
    for spot in range(2 * NX):
        wz[spot, 64:, 256:] = wz[spot, :64, :256]

    def outward(rows_of, number):
        peer = around_me[number]
        spot = peer["x"] * 2 + peer["c"]
        mark = y * 8 + here
        return sent(
            terms.at[spot, rows_of], terms_in.at[mark], fs.at[rows_of, number], fr.at[mark], {"y": rows_of, **peer}
        )

    for turn in (0, 1, 3, 2):
        rows_of = around(lax.div(z, NX) + turn, NY)
        for i in range(4):
            slot = rows_of * 4 + i
            hop = around(z - slot + NZ, NZ)
            if turn == 0:

                @pl.when(hop != 0)
                def _(slot=slot, hop=hop):
                    arrived(merged.at[slot], mr.at[hop])
            else:
                arrived(merged.at[slot], mr.at[hop])
        rows = merged[pl.ds(rows_of * 4, 4)].reshape(2, 32, 256)
        rows = jnp.concatenate([rows[0], rows[1]], axis=1)
        for spot in range(2 * NX):
            term = lax.dot_general(rows, wz[spot], (((1,), (1,)), ((), ())), preferred_element_type=jnp.float32)
            terms[spot, rows_of] = term.astype(TERM)

        @pl.when(rows_of != y)
        def _(rows_of=rows_of):
            outward(rows_of, 0).start()

        for number in range(1, 8):
            outward(rows_of, number).start()
    total = terms[here, y].astype(jnp.float32)
    for j in range(NY):
        for peer in ([] if j == 0 else [{"x": x, "c": c}]) + near:
            mark = around(y + j, NY) * 8 + peer["x"] * 2 + peer["c"]
            arrived(terms_in.at[mark], fr.at[mark])
            total = total + terms_in[mark].astype(jnp.float32)
    lines[pl.ds(0, 32, stride=2), :] = total
    lines[pl.ds(1, 32, stride=2), :] = jnp.concatenate([total[:, 64:], total[:, :64]], axis=1)
    result[...] = lines[:, :64].astype(jnp.bfloat16)
    for copy in started:
        copy.wait_send()
    for rows_of in range(NY):

        @pl.when(rows_of != y)
        def _(rows_of=rows_of):
            outward(rows_of, 0).wait_send()

        for number in range(1, 8):
            outward(rows_of, number).wait_send()
    for slot in range(NZ):

        @pl.when(z != slot)
        def _(slot=slot):
            for copy in along(slot):
                copy.wait_send()


def step(select, table, block_page, q, k, v, w):
    anywhere = pl.BlockSpec(memory_space=pl.ANY)
    inside = pl.BlockSpec(memory_space=VMEM)
    half = lambda *shape: pltpu.VMEM(shape, jnp.bfloat16)
    full = lambda *shape: pltpu.VMEM(shape, jnp.float32)
    pages = (PAGES_DEV, 2 * PAGE, HEAD)
    return pl.pallas_call(
        step_kernel,
        out_shape=jax.ShapeDtypeStruct((64, 64), jnp.bfloat16),
        in_specs=[anywhere] * 7,
        out_specs=inside,
        scratch_shapes=[
            pltpu.SMEM(select.shape, jnp.int32),
            pltpu.SMEM(table.shape, jnp.int32),
            pltpu.SMEM(block_page.shape, jnp.int32),
            pltpu.SMEM((BLOCKS * 2 * 8,), jnp.int32),
            half(2, 16, HEAD),
            half(NX, NZ, 2, 16, HEAD),
            half(*pages), half(*pages), half(*pages), half(*pages),
            full(4, 2 * PAGE, HEAD),
            half(4, KEYS, HEAD), half(4, KEYS, 2 * HEAD),
            full(512, HEAD), full(512, HEAD),
            half(NX, NZ, 16, 256), full(NX, NX, 8, HEAD),
            half(NX - 1, NZ, 16, 256), full(NX - 1, NX, 8, HEAD),
            half(NZ, 16, 256), full(NZ, 8, HEAD),
            half(NZ, 16, 256), full(NZ, 8, HEAD),
            half(NZ, 16, 256),
            half(2 * NX, 128, 512),
            pltpu.VMEM((2 * NX, NY, 32, 128), TERM),
            pltpu.VMEM((8 * NY, 32, 128), TERM),
            full(64, 128),
            DMA((8,)), DMA((2,)), DMA((2,)),
            DMA((NZ, 2)), DMA((NZ, 2)), DMA((NX - 1, NZ)), DMA((NX - 1, NZ)),
            DMA((7,)), DMA((8,)),
            DMA((NX - 1, NX)), DMA((NX - 1, NX)), DMA((NX - 1, NX)), DMA((NX - 1, NX)),
            DMA((NZ,)), DMA((NZ,)), DMA((NZ,)), DMA((NZ,)),
            DMA((NZ,)), DMA((NZ,)),
            DMA((NY, 8)), DMA((32,)),
        ],
        compiler_params=pltpu.CompilerParams(collective_id=0, has_side_effects=True),
        name="step",
    )(select, table, block_page, q, k, v, w)


def per_device(queries, cached_keys, cached_values, out_weight, select, page_table, block_page):
    q = queries.reshape(2, 2 * HEADS, HEAD).transpose(1, 0, 2).reshape(2, 16, HEAD)
    k = cached_keys.reshape(PAGES_DEV, 2 * PAGE, HEAD)
    v = cached_values.reshape(PAGES_DEV, 2 * PAGE, HEAD)
    return step(select, page_table, block_page, q, k, v, out_weight.T)


def solution(mesh):
    torus = Mesh(mesh.devices.reshape(NX, NZ, 2, NY), ("x", "z", "c", "y"))
    return jax.shard_map(
        per_device,
        mesh=torus,
        in_specs=(
            P(PAGES, "y"),
            P(PAGES, None, "y", None),
            P(PAGES, None, "y", None),
            P("y", PAGES),
            P(),
            P(),
            P(),
        ),
        out_specs=P("y", PAGES),
        check_vma=False,
    )
```

```python
import jax
import jax.numpy as jnp
from jax import lax
from jax.experimental import pallas as pl
from jax.experimental.pallas import tpu as pltpu
from jax.sharding import Mesh
from jax.sharding import PartitionSpec as P

PAGES = ("x", "z", "c")
MESH = pl.DeviceIdType.MESH
NX, NZ, NY = 4, 16, 4
REACH = NZ // 4
PAGE = 128
PAGES_DEV = 16
PICKED = 6
BLOCKS = 2
HEADS = 8
HEAD = 128
KEYS = PICKED * PAGE
SCALE = HEAD ** -0.5
SCALE2 = SCALE * 1.4426950408889634
FLOOR = -1e30
VMEM = pltpu.MemorySpace.VMEM
DMA = pltpu.SemaphoreType.DMA
TERM = jnp.bfloat16


def around(value, size):
    return lax.rem(value + size, size)


def place():
    return tuple(lax.axis_index(axis) for axis in ("x", "z", "c", "y"))


def greet(peers):
    barrier = pltpu.get_barrier_semaphore()
    for peer in peers:
        pl.semaphore_signal(barrier, inc=1, device_id=peer, device_id_type=MESH)
    return lambda: pl.semaphore_wait(barrier, len(peers))


def sent(source, target, send_sem, recv_sem, peer):
    return pltpu.make_async_remote_copy(
        src_ref=source,
        dst_ref=target,
        send_sem=send_sem,
        recv_sem=recv_sem,
        device_id=peer,
        device_id_type=MESH,
    )


def arrived(target, sem):
    pltpu.make_async_copy(target, target, sem).wait()


def nearest(reverse=False):
    found = [hop for step in range(1, NZ // 2) for hop in (step, NZ - step)] + [NZ // 2]
    return found[::-1] if reverse else found


def weighed(levels):
    top = levels[0]
    for level in levels[1:]:
        top = jnp.maximum(top, level)
    shares = [jnp.exp(level - top) for level in levels]
    total = shares[0]
    for share in shares[1:]:
        total = total + share
    scale = 1.0 / total
    return [share * scale for share in shares], top + jnp.log(total)


def mixed_by(values, shares, base):
    lines = []
    for band in range(2):
        line = []
        for half in range(2):
            lane = base + 8 * (band * 2 + half)
            total = None
            for value, share in zip(values, shares):
                term = value[band * 8:(band + 1) * 8, half * HEAD:(half + 1) * HEAD] * share[:, lane:lane + 1]
                total = term if total is None else total + term
            line.append(total)
        lines.append(jnp.concatenate(line, axis=1))
    return jnp.concatenate(lines, axis=0)


def listed(select, table, block_page, lists, chip, c):
    for block in range(BLOCKS):
        own_page = block_page[block]
        own_row = table[own_page]
        for side in range(2):
            owner = chip * 2 + (c if side == 0 else 1 - c)
            has_own = (lax.shift_right_logical(own_row, 4) == owner).astype(jnp.int32)
            spots = [jnp.where(has_own == 1, own_row & (PAGES_DEV - 1), 0)] + [jnp.int32(0)] * (PICKED - 1)

            def scan(i, carry, block=block, owner=owner, own_page=own_page):
                count, *spots = carry
                page = select[block, i]
                row = table[page]
                hit = jnp.logical_and(lax.shift_right_logical(row, 4) == owner, page != own_page)
                spots = [
                    jnp.where(jnp.logical_and(hit, count == n), row & (PAGES_DEV - 1), spot)
                    for n, spot in enumerate(spots)
                ]
                return (count + hit.astype(jnp.int32), *spots)

            count, *spots = lax.fori_loop(0, 4 * PICKED, scan, (has_own, *spots))
            base = (block * 2 + side) * 8
            for n, spot in enumerate(spots):
                lists[base + n] = spot
            lists[base + PICKED] = count
            lists[base + PICKED + 1] = has_own


def step_kernel(
    select_in, table_in, block_page_in, q_in, k, v, w, result,
    select, table, block_page, lists, q, qall, knear, vnear, kfar, vfar, flat, keys, values, acc, tops,
    part, stat, got, got_stat, send, send_stat, land, land_stat, merged, wz, terms, terms_in, lines,
    ls, ps, pr, zs, zr, xs, xr, ws, wr, gs, gr, hs, hr, rs, rr, ts, tr, ms, mr, fs, fr,
):
    x, z, c, y = place()
    here = x * 2 + c
    other = {"c": 1 - c}
    xpeers = [{"x": around(x + j, NX)} for j in range(1, NX)]
    around_me = [{"x": around(x + j, NX), "c": lax.rem(c + d, 2)} for j in range(NX) for d in range(2)]
    near = around_me[1:]
    close = nearest()[2 * REACH - 1::-1]
    peers = [{"z": around(z + hop, NZ), "c": core} for hop in close for core in range(2)] + near
    for j in range(1, NY):
        for peer in around_me:
            peers.append({"y": around(y + j, NY), **peer})
    wait_for_all = greet(peers)
    mine = pl.multiple_of((c * NX + x) * 256, 256)
    own = [
        pltpu.make_async_copy(select_in, select, ls.at[0]),
        pltpu.make_async_copy(table_in, table, ls.at[1]),
        pltpu.make_async_copy(block_page_in, block_page, ls.at[2]),
        pltpu.make_async_copy(q_in, q, ls.at[3]),
        pltpu.make_async_copy(k, knear, ls.at[4]),
        pltpu.make_async_copy(v, vnear, ls.at[5]),
        pltpu.make_async_copy(w.at[:, pl.ds(mine, 256)], wz.at[here, pl.ds(0, 64), pl.ds(0, 256)], ls.at[6]),
    ]
    for copy in own:
        copy.start()
    own[3].wait()
    copy = pltpu.make_async_copy(q.at[c], qall.at[x, z, c], ls.at[7])
    copy.start()
    own.append(copy)
    started = []

    def go(copy):
        copy.start()
        started.append(copy)

    def across(slot, number):
        for j in range(1, NX):
            go(sent(qall.at[x, slot], qall.at[x, slot], xs.at[j - 1, number], xr.at[j - 1, slot], xpeers[j - 1]))

    def untangle(side, raws):
        def one(i, _, side=side):
            for block in range(BLOCKS):
                row = lists[(block * 2 + side) * 8 + i]
                at = pl.ds(pl.multiple_of(i * PAGE, PAGE), PAGE)
                for n, (raw, kept) in enumerate(zip(raws, (keys, values))):
                    spot = block * 2 + n
                    flat[spot] = raw[row].astype(jnp.float32)
                    kept[block * 2 + side, at, :HEAD] = flat[spot, pl.ds(c, PAGE, stride=2), :].astype(jnp.bfloat16)
            return 0

        lax.fori_loop(0, PICKED, one, 0)

    wait_for_all()
    for hop in close:
        for core in range(2):
            peer = {"z": around(z + hop, NZ), "c": core}
            go(sent(q.at[core], qall.at[x, z, c], zs.at[hop, core], zr.at[hop, c], peer))
    go(sent(q.at[1 - c], qall.at[x, z, c], zs.at[0, 0], zr.at[0, c], other))
    own[4].wait()
    own[5].wait()
    go(sent(knear, kfar, ps.at[0], pr.at[0], other))
    go(sent(vnear, vfar, ps.at[1], pr.at[1], other))
    for number, peer in enumerate(near):
        theirs = pl.multiple_of((peer["c"] * NX + peer["x"]) * 256, 256)
        target = wz.at[here, pl.ds(0, 64), pl.ds(0, 256)]
        go(sent(w.at[:, pl.ds(theirs, 256)], target, ws.at[number], wr.at[here], peer))
    for copy in own[:3] + own[6:]:
        copy.wait()
    zero = jnp.zeros((2 * NX, 64, 256), jnp.bfloat16)
    wz[:, :64, 256:] = zero
    wz[:, 64:, :256] = zero
    values[:, :, HEAD:] = jnp.ones((4, KEYS, HEAD), jnp.bfloat16)
    listed(select, table, block_page, lists, x * NZ + z, c)
    def came(hop):
        slot = around(z - hop, NZ)
        for core in range(2):
            arrived(qall.at[x, slot, core], zr.at[hop, core])
        return slot

    for sign in (1, -1):
        slot = came(REACH if sign == 1 else NZ - REACH)
        for leg in range(REACH if sign == 1 else REACH - 1, 0, -1):
            hop = sign * (REACH + leg) % NZ
            go(sent(
                qall.at[x, slot], qall.at[x, slot], zs.at[hop, 0], zr.at[hop, 0], {"z": around(z + sign * leg, NZ)}
            ))
    arrived(qall.at[x, z, 1 - c], zr.at[0, 1 - c])
    across(z, 0)
    for number, hop in enumerate(nearest()[:2 * REACH]):
        if hop in (REACH, NZ - REACH):
            slot = around(z - hop, NZ)
        else:
            slot = came(hop)
        across(slot, 1 + number)
    untangle(0, (knear, vnear))
    for number, hop in enumerate(nearest()[2 * REACH:]):
        slot = around(z - hop, NZ)
        arrived(qall.at[x, slot], zr.at[hop, 0])
        across(slot, 1 + 2 * REACH + number)
    arrived(kfar, pr.at[0])
    arrived(vfar, pr.at[1])
    untangle(1, (kfar, vfar))
    lane = lax.broadcasted_iota(jnp.int32, (8, HEAD), 1)
    size = 256

    def group(xg):
        block = xg // 2
        away = around(x - xg, NX)

        @pl.when(away != 0)
        def _():
            for slot in range(NZ):
                arrived(qall.at[xg, slot], xr.at[away - 1, slot])

        for tile in range(2):
            rows = pl.ds(tile * size, size)
            queries = qall[xg, tile * 8:tile * 8 + 8].reshape(size, HEAD)
            sides = []
            for side in range(2):
                combo = block * 2 + side
                scores = lax.dot_general(
                    queries, keys[combo], (((1,), (1,)), ((), ())), preferred_element_type=jnp.float32
                )
                slack = jnp.where(lists[combo * 8 + PICKED + 1] == 1, 0, PAGE)
                line = lax.broadcasted_iota(jnp.int32, (size, PAGE), 0) + tile * size
                row = lax.shift_left(lax.shift_right_logical(line, 4), 1) + (line & 1) + xg % 2 * 64
                key = lax.broadcasted_iota(jnp.int32, (size, PAGE), 1)
                first = jnp.where(key <= row + slack, scores[:, :PAGE], FLOOR)
                scores = jnp.concatenate([first, scores[:, PAGE:]], axis=1)
                peak = jnp.max(scores, axis=1, keepdims=True)
                weights = jnp.exp2((scores - peak) * SCALE2)
                both = jnp.dot(weights.astype(jnp.bfloat16), values[combo], preferred_element_type=jnp.float32)
                out, total = both[:, :HEAD], both[:, HEAD:HEAD + 1]
                level = peak * SCALE + jnp.log(total)
                level = jnp.where(lists[combo * 8 + PICKED] == PICKED, level, FLOOR)
                sides.append((out, total, level))
            top = jnp.maximum(sides[0][2], sides[1][2])
            shares = [jnp.exp(level - top) for _, _, level in sides]
            whole = shares[0] + shares[1]
            acc[rows, :] = sum(
                out * (share / (whole * total)) for (out, total, _), share in zip(sides, shares)
            )
            tops[rows, :] = jnp.broadcast_to(top + jnp.log(whole), (size, HEAD))
        for xd in range(NX):
            tile = None
            for r in range(2):
                at = slice(4 * xg + 2 * r, 4 * xg + 2 * r + 2)
                pieces = []
                for half in range(2):
                    start = (2 * xd + half) * 2 + r
                    piece = acc[pl.ds(start, 32, stride=16), :].astype(jnp.bfloat16)
                    part[xd, at, :, half * HEAD:(half + 1) * HEAD] = piece.reshape(2, 16, HEAD)
                    pieces.append(tops[pl.ds(start, 32, stride=16), :])
                for spot in range(8):
                    top = pieces[spot % 2][spot // 2 * 8:spot // 2 * 8 + 8]
                    tile = top if tile is None else jnp.where(lane >= r * 64 + spot * 8, top, tile)
            stat[xd, xg] = tile
        at = pl.ds(4 * xg, 4)
        for j in range(1, NX):
            xd = around(x + j, NX)
            go(sent(stat.at[xd, xg], got_stat.at[j - 1, xg], hs.at[j - 1, xg], hr.at[j - 1, xg], xpeers[j - 1]))
            go(sent(part.at[xd, at], got.at[j - 1, at], gs.at[j - 1, xg], gr.at[j - 1, xg], xpeers[j - 1]))

    def along(slot):
        peer = {"z": jnp.int32(slot)}
        return [
            sent(send_stat.at[slot], land_stat.at[z], ts.at[slot], tr.at[z], peer),
            sent(send.at[slot], land.at[z], rs.at[slot], rr.at[z], peer),
        ]

    def combine(xg):
        for j in range(NX - 1):
            arrived(got_stat.at[j, xg], hr.at[j, xg])
            arrived(got.at[j, pl.ds(4 * xg, 4)], gr.at[j, xg])
        shares, level = weighed([stat[x, xg]] + [got_stat[j, xg] for j in range(NX - 1)])
        for i in range(4):
            slot = 4 * xg + i
            items = [part[x, slot]] + [got[j, slot] for j in range(NX - 1)]
            value = mixed_by([item.astype(jnp.float32) for item in items], shares, 32 * i)
            turned = pltpu.roll(level, 128 - 32 * i, 1) if i else level

            @pl.when(z == slot)
            def _(value=value, turned=turned):
                land[z] = value.astype(jnp.bfloat16)
                land_stat[z] = turned

            @pl.when(z != slot)
            def _(value=value, turned=turned, slot=slot):
                send[slot] = value.astype(jnp.bfloat16)
                send_stat[slot] = turned
                for copy in along(slot):
                    copy.start()

    group(0)
    group(1)
    combine(0)
    group(2)
    combine(1)
    group(3)
    combine(2)
    combine(3)
    for hop in nearest():
        slot = around(z - hop, NZ)
        arrived(land_stat.at[slot], tr.at[slot])
        arrived(land.at[slot], rr.at[slot])
    shares, _ = weighed([land_stat[slot] for slot in range(NZ)])
    merged[z] = mixed_by([land[slot].astype(jnp.float32) for slot in range(NZ)], shares, 0).astype(jnp.bfloat16)
    for hop in nearest(True):
        go(sent(merged.at[z], merged.at[z], ms.at[hop], mr.at[hop], {"z": around(z + hop, NZ)}))
    for peer in near:
        there = peer["x"] * 2 + peer["c"]
        arrived(wz.at[there, pl.ds(0, 64), pl.ds(0, 256)], wr.at[there])
    for spot in range(2 * NX):
        wz[spot, 64:, 256:] = wz[spot, :64, :256]

    def outward(rows_of, number):
        peer = around_me[number]
        spot = peer["x"] * 2 + peer["c"]
        mark = y * 8 + here
        return sent(
            terms.at[spot, rows_of], terms_in.at[mark], fs.at[rows_of, number], fr.at[mark], {"y": rows_of, **peer}
        )

    for turn in (0, 1, 3, 2):
        rows_of = around(lax.div(z, NX) + turn, NY)
        for i in range(4):
            slot = rows_of * 4 + i
            hop = around(z - slot + NZ, NZ)
            if turn == 0:

                @pl.when(hop != 0)
                def _(slot=slot, hop=hop):
                    arrived(merged.at[slot], mr.at[hop])
            else:
                arrived(merged.at[slot], mr.at[hop])
        rows = merged[pl.ds(rows_of * 4, 4)].reshape(2, 32, 256)
        rows = jnp.concatenate([rows[0], rows[1]], axis=1)
        for spot in range(2 * NX):
            term = lax.dot_general(rows, wz[spot], (((1,), (1,)), ((), ())), preferred_element_type=jnp.float32)
            terms[spot, rows_of] = term.astype(TERM)

        @pl.when(rows_of != y)
        def _(rows_of=rows_of):
            outward(rows_of, 0).start()

        for number in range(1, 8):
            outward(rows_of, number).start()
    total = terms[here, y].astype(jnp.float32)
    for j in range(NY):
        for peer in ([] if j == 0 else [{"x": x, "c": c}]) + near:
            mark = around(y + j, NY) * 8 + peer["x"] * 2 + peer["c"]
            arrived(terms_in.at[mark], fr.at[mark])
            total = total + terms_in[mark].astype(jnp.float32)
    lines[pl.ds(0, 32, stride=2), :] = total
    lines[pl.ds(1, 32, stride=2), :] = jnp.concatenate([total[:, 64:], total[:, :64]], axis=1)
    result[...] = lines[:, :64].astype(jnp.bfloat16)
    for copy in started:
        copy.wait_send()
    for rows_of in range(NY):

        @pl.when(rows_of != y)
        def _(rows_of=rows_of):
            outward(rows_of, 0).wait_send()

        for number in range(1, 8):
            outward(rows_of, number).wait_send()
    for slot in range(NZ):

        @pl.when(z != slot)
        def _(slot=slot):
            for copy in along(slot):
                copy.wait_send()


def step(select, table, block_page, q, k, v, w):
    anywhere = pl.BlockSpec(memory_space=pl.ANY)
    inside = pl.BlockSpec(memory_space=VMEM)
    half = lambda *shape: pltpu.VMEM(shape, jnp.bfloat16)
    full = lambda *shape: pltpu.VMEM(shape, jnp.float32)
    pages = (PAGES_DEV, 2 * PAGE, HEAD)
    return pl.pallas_call(
        step_kernel,
        out_shape=jax.ShapeDtypeStruct((64, 64), jnp.bfloat16),
        in_specs=[anywhere] * 7,
        out_specs=inside,
        scratch_shapes=[
            pltpu.SMEM(select.shape, jnp.int32),
            pltpu.SMEM(table.shape, jnp.int32),
            pltpu.SMEM(block_page.shape, jnp.int32),
            pltpu.SMEM((BLOCKS * 2 * 8,), jnp.int32),
            half(2, 16, HEAD),
            half(NX, NZ, 2, 16, HEAD),
            half(*pages), half(*pages), half(*pages), half(*pages),
            full(4, 2 * PAGE, HEAD),
            half(4, KEYS, HEAD), half(4, KEYS, 2 * HEAD),
            full(512, HEAD), full(512, HEAD),
            half(NX, NZ, 16, 256), full(NX, NX, 8, HEAD),
            half(NX - 1, NZ, 16, 256), full(NX - 1, NX, 8, HEAD),
            half(NZ, 16, 256), full(NZ, 8, HEAD),
            half(NZ, 16, 256), full(NZ, 8, HEAD),
            half(NZ, 16, 256),
            half(2 * NX, 128, 512),
            pltpu.VMEM((2 * NX, NY, 32, 128), TERM),
            pltpu.VMEM((8 * NY, 32, 128), TERM),
            full(64, 128),
            DMA((8,)), DMA((2,)), DMA((2,)),
            DMA((NZ, 2)), DMA((NZ, 2)), DMA((NX - 1, NZ)), DMA((NX - 1, NZ)),
            DMA((7,)), DMA((8,)),
            DMA((NX - 1, NX)), DMA((NX - 1, NX)), DMA((NX - 1, NX)), DMA((NX - 1, NX)),
            DMA((NZ,)), DMA((NZ,)), DMA((NZ,)), DMA((NZ,)),
            DMA((NZ,)), DMA((NZ,)),
            DMA((NY, 8)), DMA((32,)),
        ],
        compiler_params=pltpu.CompilerParams(collective_id=0, has_side_effects=True),
        name="step",
    )(select, table, block_page, q, k, v, w)


def per_device(queries, cached_keys, cached_values, out_weight, select, page_table, block_page):
    q = queries.reshape(2, 2 * HEADS, HEAD).transpose(1, 0, 2).reshape(2, 16, HEAD)
    k = cached_keys.reshape(PAGES_DEV, 2 * PAGE, HEAD)
    v = cached_values.reshape(PAGES_DEV, 2 * PAGE, HEAD)
    return step(select, page_table, block_page, q, k, v, out_weight.T)


def solution(mesh):
    torus = Mesh(mesh.devices.reshape(NX, NZ, 2, NY), ("x", "z", "c", "y"))
    return jax.shard_map(
        per_device,
        mesh=torus,
        in_specs=(
            P(PAGES, "y"),
            P(PAGES, None, "y", None),
            P(PAGES, None, "y", None),
            P("y", PAGES),
            P(),
            P(),
            P(),
        ),
        out_specs=P("y", PAGES),
        check_vma=False,
    )
```
